32 devices in a mesh: grp: 2 (over y), var: 16 (over z, x, core).
Axes of the slice: x: 2, y: 2, z: 4, core: 2. Of those that a mesh axis runs over, the one named last changes fastest.
Arguments:
- genotypes: int32 [256, 61440], P('grp', 'var'), parts along dimension 0, may hold values from 0 to 2
- labels: int32 [256], P('grp'), parts along dimension 0, may hold values 0 or 1
- gene_weight: bfloat16 [480, 128, 128], P('var'), may hold values from -0.375 to 0.375
- gene_idx: int32 [480, 8], replicated, may hold values from 0 to 2559, as said below
- head_weight: float32 [2560, 16], P('var'), may hold values from -0.0625 to 0.0625
- head_bias: float32 [1], replicated, may hold values from -1 to 1
Outputs:
- grad_w: float32 [960, 128, 128], P(('grp', 'var')), parts along dimension 0
- grad_head: float32 [5120, 16], P(('grp', 'var')), parts along dimension 0
- totals: float32 [4], P('grp'), parts along dimension 0
The draws below stay inside these ranges and needn't reach their ends.
There are 2 independent parts, one for each index of `grp`. The reference program is written for one: setup_inputs(seed, part) draws one part's arguments, and reference() takes and returns one part's arrays. A program takes and returns all parts, laid end to end along the dimension named above; an argument that names none is the same for every part. Nothing has to cross between parts.
Inputs may be any that keep to these rules, and one draw needn't show every extreme that they name: `gene_idx`: device d's edges (its 30 blocks times 8 slots, block-major) name genes d * 160 to (d + 1) * 160 - 1, except at most 32 leading edges that name some of the last 8 genes of device d - 1 and at most 32 trailing edges that name some of the first 8 genes of device d + 1; the first device has no leading and the last no trailing ones; the first device has exactly 32 trailing edges, naming 8 genes; every gene is named.
All inputs are finite; a program needn't handle non-finite values.
Results may differ from the reference program's by a relative error of at most 0.0036.
Values may be sent and summed in bfloat16 or wider, within the bound.
A program may use at most 64 MiB of HBM per device.

```python
import jax
import jax.numpy as jnp
from jax import lax

CH = 16
BLOCK = 128
SLOTS = 8
BLK_DEV = 30
G_DEV = 160
GSTR = 8
CAP = 32
SAMP = 128
BLOCKS = 480
VARIANTS = 61440
GENES = 2560


def draw_gene_idx(key, part):
    devices = BLOCKS // BLK_DEV
    edges = BLK_DEV * SLOTS
    first_key, second_key, third_key = jax.random.split(key, 3)
    lower = jax.random.randint(first_key, (devices,), 0, CAP + 1)
    upper = jax.random.randint(second_key, (devices,), 0, CAP + 1)
    filled = jax.random.randint(third_key, (), 0, devices)
    marks = jnp.arange(devices, dtype=jnp.int32)
    lower = jnp.where(marks == filled, CAP, lower)
    upper = jnp.where(marks == filled, CAP, upper)
    upper = jnp.where(marks == 0, CAP, upper)
    lower = jnp.where(marks == 0, 0, lower)
    upper = jnp.where(marks == devices - 1, 0, upper)
    position = jnp.arange(edges, dtype=jnp.int32)[None, :]
    lower_n = lower[:, None]
    upper_n = upper[:, None]
    owner = marks[:, None]
    own_count = edges - lower_n - upper_n
    own_gene = owner * G_DEV + (position - lower_n) * G_DEV // own_count
    lower_span = jnp.minimum(lower_n, GSTR)
    lower_gene = owner * G_DEV - lower_span + position * lower_span // jnp.maximum(lower_n, 1)
    upper_span = jnp.minimum(upper_n, GSTR)
    upper_gene = (owner + 1) * G_DEV + (position - (edges - upper_n)) * upper_span // jnp.maximum(upper_n, 1)
    genes = jnp.where(position < lower_n, lower_gene, jnp.where(position >= edges - upper_n, upper_gene, own_gene))
    return genes.reshape(BLOCKS, SLOTS).astype(jnp.int32)


def plant(drawn, key, low, high):
    shape = drawn.shape
    place = [jax.random.randint(jax.random.fold_in(key, axis), (), 0, shape[axis]) for axis in range(len(shape))]
    drawn = drawn.at[tuple(place)].set(low)
    longest = shape.index(max(shape))
    place[longest] = (place[longest] + 1) % shape[longest]
    return drawn.at[tuple(place)].set(high)


def shard_levels(stream_key, shape, cuts, least, largest):
    loudness, own = 1.0, jax.random.fold_in(stream_key, 6)
    for axis_at, parts in cuts:
        heights = jnp.exp(jax.random.uniform(jax.random.fold_in(own, axis_at), (parts,), jnp.float32, least / len(cuts), largest / len(cuts)))
        loudness = loudness * jnp.repeat(heights, shape[axis_at] // parts).reshape([-1 if axis == axis_at else 1 for axis in range(len(shape))])
    return loudness


def normal_values(rng, dims, spread, most, pieces=(), kind=jnp.bfloat16):
    loudness = shard_levels(rng, dims, pieces, -0.22, 0.18) if pieces else 1.0
    drawn = jax.random.normal(rng, dims, jnp.float32) * spread * loudness
    return jnp.minimum(jnp.maximum(drawn, -most), most).astype(kind)


def setup_inputs(seed: int = 0, part: int = 0) -> dict:
    splits = jax.random.split(jax.random.key(seed), 7)
    part_keys = jax.random.split(jax.random.fold_in(splits[6], part), 7)
    return {
        "genotypes": plant(jax.random.randint(part_keys[0], (SAMP, VARIANTS), 0, 3), jax.random.fold_in(part_keys[0], 1), 0, 2).astype(jnp.int32),
        "labels": plant((jax.random.randint(part_keys[1], (SAMP,), 0, 2) < 1).astype(jnp.int32), jax.random.fold_in(part_keys[1], 1), 0, 1),
        "gene_weight": normal_values(splits[2], (BLOCKS, BLOCK, SLOTS * CH), (2 * BLOCK) ** -0.5, 0.375, ((0, 16),)),
        "gene_idx": draw_gene_idx(jax.random.fold_in(splits[6], 71), part),
        "head_weight": normal_values(splits[4], (GENES, CH), (GENES * CH // 4) ** -0.5, 0.0625, ((0, 16),), jnp.float32),
        "head_bias": jnp.clip(jax.random.uniform(splits[5], (1,), jnp.float32, -1.0, 1.0), -1.0, 1.0),
    }


root_half = 0.7071067811865476
inv_root_tau = 0.3989422804014327

def gelu_parts(values):
    normal_cdf = 0.5 * (1.0 + lax.erf(values * root_half))
    return (values * normal_cdf, normal_cdf + values * jnp.exp(-0.5 * values * values) * inv_root_tau)

def reference(genotypes, labels, gene_weight, gene_idx, head_weight, head_bias):
    samples = genotypes.shape[0]
    dosage = jnp.swapaxes(genotypes.reshape(samples, BLOCKS, BLOCK), 0, 1).astype(jnp.bfloat16)

    def add_block(total, inputs):
        block_dose, weight, slot_ids = inputs
        part = jnp.dot(block_dose, weight, preferred_element_type=jnp.float32).reshape(samples, SLOTS, CH)
        return (total.at[:, slot_ids, :].add(part), None)
    start = jnp.zeros((samples, GENES, CH), jnp.float32)
    gene_sum, _ = lax.scan(add_block, start, (dosage, gene_weight, gene_idx))
    activation, slopes = gelu_parts(gene_sum)
    logits = jnp.einsum('sgc,gc->s', activation, head_weight, precision=lax.Precision.HIGHEST) + head_bias[0]
    targets = labels.astype(jnp.float32)
    total_loss = jnp.sum(jax.nn.softplus(logits) - targets * logits)
    dlogit = jax.nn.sigmoid(logits) - targets
    grad_bias = jnp.sum(dlogit)
    grad_head = jnp.einsum('s,sgc->gc', dlogit, activation, precision=lax.Precision.HIGHEST)
    grad_gene = (dlogit[:, None, None] * head_weight[None, :, :] * slopes).astype(jnp.bfloat16)

    def block_grad(inputs):
        block_dose, slot_ids = inputs
        picked = grad_gene[:, slot_ids, :].reshape(samples, SLOTS * CH)
        return jnp.dot(block_dose.T, picked, preferred_element_type=jnp.float32)
    grad_w = lax.map(block_grad, (dosage, gene_idx))
    return (grad_w, grad_head, jnp.stack([total_loss, grad_bias]))
```

```python
import functools

import jax
import jax.numpy as jnp
from jax import lax
from jax.experimental import pallas as pl
from jax.experimental.pallas import tpu as pltpu
from jax.sharding import PartitionSpec as P

CH = 16
BLOCK = 128
SLOTS = 8
GSTR = 8
CAP = 32
OUT_PARTS = (2, 6, 12, 18, 24, 30)

root_half = 0.7071067811865476
inv_root_tau = 0.3989422804014327

MESH = pl.DeviceIdType.MESH
F32 = jnp.float32
BF16 = jnp.bfloat16
NT = (((1,), (1,)), ((), ()))


def split_blocks(blocks):
    end = CAP // SLOTS
    inner = blocks - 2 * end
    cuts = [end + inner * k // 4 for k in range(5)]
    return [(0, end), (blocks - end, end)] + [(p, q - p) for p, q in zip(cuts, cuts[1:])]


def forward_kernel(
    n, ids_hbm, hw_hbm, geno_hbm, w_hbm,
    dose_ref, turned_ref, act_ref, logit_ref,
    spread_ref, ids_ref, hw_ref, geno, weight, dosage, hs_ref, cdfs, sums, given, taken, lending, lent, mine, shares,
    geno_sem, w_sem, small_sem, halo_send, halo_recv, own_send, own_recv, share_send, share_recv,
):
    me = lax.axis_index("var")
    samples = geno.shape[0]
    blocks = weight.shape[0]
    genes = hw_ref.shape[1]
    rows = genes + 2 * GSTR
    edges = blocks * SLOTS
    all_blocks = ids_ref.shape[1]
    edge = 2 * GSTR

    barrier = pltpu.get_barrier_semaphore()

    pieces = split_blocks(blocks)

    def geno_copy(i):
        first, count = pieces[i]
        cols = pl.ds(first * BLOCK, count * BLOCK)
        return pltpu.make_async_copy(geno_hbm.at[:, cols], geno.at[:, cols], geno_sem.at[i])

    def w_copy(i):
        at = pl.ds(*pieces[i])
        return pltpu.make_async_copy(w_hbm.at[at], weight.at[at], w_sem.at[i])

    ids_copy = pltpu.make_async_copy(ids_hbm, ids_ref, small_sem.at[0])
    hw_load = pltpu.make_async_copy(hw_hbm, hw_ref, small_sem.at[1])
    ids_copy.start()
    for i in range(len(pieces)):
        geno_copy(i).start()
        w_copy(i).start()
        if i == 1:
            def greet(j):
                pl.semaphore_signal(
                    barrier, inc=1, device_id={"var": lax.rem(me + j, n)}, device_id_type=MESH
                )

            greet(n - 1)
            greet(1)

            @pl.loop(2, n - 1)
            def _(j):
                greet(j)
    hw_load.start()

    part = spread_ref

    def do_chunk(i):
        geno_copy(i).wait()
        w_copy(i).wait()
        for b in range(pieces[i][0], sum(pieces[i])):
            at = pl.ds(b * BLOCK, BLOCK)
            dose = geno[:, at].astype(F32).astype(BF16)
            dosage[:, at] = dose
            part[at, :] = lax.dot_general(
                weight[b], dose, (((0,), (1,)), ((), ())), preferred_element_type=F32
            )

    ids_copy.wait()
    first = me * genes - GSTR
    ids = ids_ref[...]
    width = -(-all_blocks // 128) * 128
    if width > all_blocks:
        ids = jnp.concatenate([ids, jnp.zeros((SLOTS, width - all_blocks), jnp.int32)], axis=1)
    near = pltpu.roll(ids, lax.rem(width - me * blocks, width), 1)[:, :128] - first
    near = near.astype(F32).astype(BF16)
    chosen = (
        lax.broadcasted_iota(jnp.int32, (edges, 128), 1)
        == lax.broadcasted_iota(jnp.int32, (edges, 128), 0) // SLOTS
    ).astype(F32).astype(BF16)
    wide = lax.dot_general(near, chosen, NT, preferred_element_type=F32)
    slot = lax.broadcasted_iota(jnp.int32, (SLOTS, edges), 0)
    lane = lax.broadcasted_iota(jnp.int32, (SLOTS, edges), 1)
    id_row = jnp.sum(jnp.where(lane % SLOTS == slot, wide, 0.0), axis=0, keepdims=True)
    id_row = id_row.astype(jnp.int32)

    id_ends = jnp.concatenate([id_row[:, :CAP], id_row[:, edges - CAP:]], axis=1)
    id_ends = jnp.concatenate([id_ends, id_ends], axis=1)
    end_at = lax.broadcasted_iota(jnp.int32, (edge, 4 * CAP), 0)
    end_at = jnp.where(end_at < GSTR, end_at, end_at + (rows - edge))
    end_summer = (end_at == id_ends).astype(F32).astype(BF16)

    do_chunk(0)
    do_chunk(1)

    for c in range(0, CH, 2):
        ends = jnp.concatenate([
            jnp.concatenate([
                part[pl.ds(c + k, CAP, stride=CH), :],
                part[pl.ds((edges - CAP) * CH + c + k, CAP, stride=CH), :],
            ], axis=0) for k in range(2)
        ], axis=1)
        high = ends.astype(BF16)
        low = (ends - high.astype(F32)).astype(BF16)
        total = jnp.dot(
            end_summer, jnp.concatenate([high, low], axis=0), preferred_element_type=F32
        )
        for side in range(2):
            these = total[side * GSTR:(side + 1) * GSTR]
            given[side, c * GSTR:(c + 2) * GSTR, :] = jnp.concatenate(
                [these[:, :samples], these[:, samples:]], axis=0
            ).astype(BF16)

    pl.semaphore_wait(barrier, n - 1)
    has_lower = me > 0
    has_upper = me < n - 1

    def neighbour(side):
        return {"var": me - 1 if side == 0 else me + 1}

    def halo_copy(side, land):
        return pltpu.make_async_remote_copy(
            src_ref=given.at[side], dst_ref=taken.at[land],
            send_sem=halo_send.at[side], recv_sem=halo_recv.at[land],
            device_id=neighbour(side), device_id_type=MESH,
        )

    def own_copy(side, land):
        return pltpu.make_async_remote_copy(
            src_ref=lending.at[side], dst_ref=lent.at[land],
            send_sem=own_send.at[side], recv_sem=own_recv.at[land],
            device_id=neighbour(side), device_id_type=MESH,
        )

    for side, there in ((0, has_lower), (1, has_upper)):
        @pl.when(there)
        def _(side=side):
            halo_copy(side, 1 - side).start()

        @pl.when(jnp.logical_not(there))
        def _(side=side):
            taken[side] = jnp.zeros(taken.shape[1:], BF16)
            lent[side] = jnp.zeros(lent.shape[1:], BF16)

    for i in range(2, len(pieces)):
        do_chunk(i)

    gene_at = lax.broadcasted_iota(jnp.int32, (rows, edges), 0)
    summer = (gene_at == id_row).astype(F32).astype(BF16)
    for c in range(0, CH, 2):
        both = jnp.concatenate(
            [part[pl.ds(c, edges, stride=CH), :], part[pl.ds(c + 1, edges, stride=CH), :]], axis=1
        )
        high = both.astype(BF16)
        low = (both - high.astype(F32)).astype(BF16)
        total = jnp.dot(summer, high, preferred_element_type=F32)
        total = total + jnp.dot(summer, low, preferred_element_type=F32)
        sums[c] = total[:, :samples]
        sums[c + 1] = total[:, samples:]

    hw_load.wait()
    hw_own = hw_ref[...].T
    share = jnp.zeros((8, samples), F32)
    inner = rows - 2 * edge

    def spread(column, count):
        return jnp.broadcast_to(column, (count, samples))

    def cdf_of(values):
        return 0.5 * (1.0 + lax.erf(values * root_half))

    def slopes_of(values, cdf):
        return cdf + values * jnp.exp(-0.5 * values * values) * inv_root_tau

    for c in range(CH):
        values = sums[c, edge:rows - edge, :]
        cdf = cdf_of(values)
        cdfs[c, GSTR:genes - GSTR, :] = cdf
        hw = spread(hw_own[GSTR:genes - GSTR, c:c + 1], inner)
        share = share + jnp.sum((values * cdf * hw).reshape(inner // 8, 8, samples), axis=0)

    for side, there in ((0, has_lower), (1, has_upper)):
        @pl.when(there)
        def _(side=side):
            halo_copy(side, side).wait()

    for c in range(CH):
        for side in range(2):
            at = GSTR if side == 0 else rows - edge
            pair = taken[side, c // 2 * 2 * GSTR:(c // 2 + 1) * 2 * GSTR, :].astype(F32)
            values = sums[c, at:at + GSTR, :] + pair[c % 2 * GSTR:(c % 2 + 1) * GSTR]
            cdf = cdf_of(values)
            sums[c, at:at + GSTR, :] = values
            cdfs[c, at - GSTR:at, :] = cdf
            share = share + values * cdf * spread(hw_own[at - GSTR:at, c:c + 1], GSTR)

    mine[0] = jnp.sum(share, axis=0, keepdims=True)

    def share_copy(other, slot):
        return pltpu.make_async_remote_copy(
            src_ref=mine.at[0], dst_ref=shares.at[slot],
            send_sem=share_send.at[other], recv_sem=share_recv.at[slot],
            device_id={"var": other}, device_id_type=MESH,
        )

    def skip_me(j):
        return j + (j >= me).astype(jnp.int32)

    @pl.loop(0, n - 1)
    def _(j):
        share_copy(skip_me(j), me).start()

    shares[me] = mine[0]

    for side in range(2):
        at = GSTR if side == 0 else rows - edge
        for c in range(0, CH, 2):
            pair = []
            for k in range(c, c + 2):
                values = sums[k, at:at + GSTR, :]
                hw = spread(hw_own[at - GSTR:at, k:k + 1], GSTR)
                pair.append(hw * slopes_of(values, cdfs[k, at - GSTR:at, :]))
            lending[side, c * GSTR:(c + 2) * GSTR, :] = jnp.concatenate(pair, axis=0).astype(BF16)

    for side, there in ((0, has_lower), (1, has_upper)):
        @pl.when(there)
        def _(side=side):
            own_copy(side, 1 - side).start()

    for c in range(CH):
        values = sums[c, GSTR:rows - GSTR, :]
        cdf = cdfs[c]
        hs_ref[c] = spread(hw_own[:, c:c + 1], genes) * slopes_of(values, cdf)
        act = values * cdf
        high = act.astype(BF16)
        act_ref[c, :, :samples] = high
        act_ref[c, :, samples:] = (act - high.astype(F32)).astype(BF16)

    for b in range(blocks):
        at = pl.ds(b * BLOCK, BLOCK)
        dose_ref[at, :] = dosage[:, at].T

    tall = lax.dot_general(chosen, near, NT, preferred_element_type=F32)
    slot = lax.broadcasted_iota(jnp.int32, (edges, SLOTS), 1)
    sub = lax.broadcasted_iota(jnp.int32, (edges, SLOTS), 0)
    id_col = jnp.sum(jnp.where(sub % SLOTS == slot, tall, 0.0), axis=1, keepdims=True)
    id_col = id_col.astype(jnp.int32)
    gene_at = lax.broadcasted_iota(jnp.int32, (edges, genes), 1) + GSTR
    pick = (gene_at == id_col).astype(F32).astype(BF16)
    id_ends = jnp.concatenate([id_col[:CAP], id_col[edges - CAP:]], axis=0)
    end_at = lax.broadcasted_iota(jnp.int32, (2 * CAP, edge), 1)
    end_at = jnp.where(end_at < GSTR, end_at, end_at + (rows - edge))
    end_pick = (end_at == id_ends).astype(F32).astype(BF16)

    for c in range(0, CH, 2):
        both = jnp.concatenate([hs_ref[c], hs_ref[c + 1]], axis=1)
        high = both.astype(BF16)
        low = (both - high.astype(F32)).astype(BF16)
        picked = jnp.dot(pick, high, preferred_element_type=F32)
        picked = picked + jnp.dot(pick, low, preferred_element_type=F32)
        spread_ref[pl.ds(c, edges, stride=CH), :] = picked[:, :samples]
        spread_ref[pl.ds(c + 1, edges, stride=CH), :] = picked[:, samples:]

    def turn(b):
        at = pl.ds(b * BLOCK, BLOCK)
        turned_ref[b] = spread_ref[at, :].T

    for b in range(CAP // SLOTS, blocks - CAP // SLOTS):
        turn(b)

    for side, there in ((0, has_lower), (1, has_upper)):
        @pl.when(there)
        def _(side=side):
            own_copy(side, side).wait()

    for c in range(0, CH, 2):
        sides = []
        for side in range(2):
            pair = lent[side, c * GSTR:(c + 2) * GSTR, :].astype(F32)
            sides.append(jnp.concatenate([pair[:GSTR], pair[GSTR:]], axis=1))
        both = jnp.concatenate(sides, axis=0).astype(BF16)
        picked = jnp.dot(end_pick, both, preferred_element_type=F32)
        for k in range(2):
            cols = slice(k * samples, (k + 1) * samples)
            for side in range(2):
                at = pl.ds(side * (edges - CAP) * CH + c + k, CAP, stride=CH)
                spread_ref[at, :] = spread_ref[at, :] + picked[side * CAP:(side + 1) * CAP, cols]

    for b in range(CAP // SLOTS):
        turn(b)
        turn(blocks - 1 - b)

    @pl.loop(0, n - 1)
    def _(j):
        other = skip_me(j)
        share_copy(other, other).wait()

    logit_ref[...] = jnp.sum(shares[...], axis=0)


def backward_kernel(
    logit_ref, labels_ref, bias_ref, dose_ref, spread_ref, act_ref,
    grad_w_hbm, grad_head_hbm, totals_hbm, out, head, totals, out_sem, small_sem,
):
    samples = dose_ref.shape[1]
    blocks = out.shape[0]
    logits = logit_ref[...] + bias_ref[...]
    targets = labels_ref[...].astype(F32)
    dlogit = jax.nn.sigmoid(logits) - targets
    tall = jnp.broadcast_to(dlogit, (samples, samples)).T
    cuts = [blocks * p // OUT_PARTS[-1] for p in (0,) + OUT_PARTS]

    def out_copy(i):
        at = pl.ds(cuts[i], cuts[i + 1] - cuts[i])
        return pltpu.make_async_copy(out.at[at], grad_w_hbm.at[at], out_sem.at[i])

    for i in range(len(OUT_PARTS)):
        for b in range(cuts[i], cuts[i + 1]):
            grad_gene = (tall * spread_ref[b]).astype(BF16)
            out[b] = jnp.dot(
                dose_ref[pl.ds(b * BLOCK, BLOCK), :], grad_gene, preferred_element_type=F32
            )
        out_copy(i).start()

    loss = jnp.maximum(logits, 0.0) + jnp.log1p(jnp.exp(-jnp.abs(logits))) - targets * logits
    totals[0] = jnp.sum(loss)
    totals[1] = jnp.sum(dlogit)
    totals_copy = pltpu.make_async_copy(totals, totals_hbm, small_sem.at[0])
    totals_copy.start()

    top = dlogit.astype(BF16).astype(F32)
    middle = (dlogit - top).astype(BF16).astype(F32)
    rest = dlogit - top - middle
    row = lax.broadcasted_iota(jnp.int32, (8, samples), 0)
    parts = jnp.where(row == 0, top, jnp.where(row == 1, middle, jnp.where(row == 2, rest, 0.0)))
    parts = jnp.concatenate([parts, parts], axis=1).astype(BF16)
    for c in range(CH):
        found = lax.dot_general(parts, act_ref[c], NT, preferred_element_type=F32)
        head[c:c + 1, :] = jnp.sum(found, axis=0, keepdims=True)
    head_copy = pltpu.make_async_copy(head, grad_head_hbm, small_sem.at[1])
    head_copy.start()
    for i in range(len(OUT_PARTS)):
        out_copy(i).wait()
    totals_copy.wait()
    head_copy.wait()


def per_device(genotypes, labels, gene_weight, gene_idx, head_weight, head_bias):
    samples = genotypes.shape[0]
    blocks = gene_weight.shape[0]
    genes = head_weight.shape[0]
    rows = genes + 2 * GSTR
    n = lax.axis_size("var")
    vmem = pl.BlockSpec(memory_space=pltpu.VMEM)
    hbm = pl.BlockSpec(memory_space=pltpu.HBM)
    shape = jax.ShapeDtypeStruct
    dma = pltpu.SemaphoreType.DMA
    pieces = len(split_blocks(blocks))
    parts = len(OUT_PARTS)
    stay = functools.partial(pltpu.with_memory_space_constraint, memory_space=pltpu.HBM)
    dose, spread, act, logit = pl.pallas_call(
        functools.partial(forward_kernel, n),
        out_shape=(
            shape((blocks * BLOCK, samples), BF16),
            shape((blocks, samples, SLOTS * CH), F32),
            shape((CH, genes, 2 * samples), BF16),
            shape((1, samples), F32),
        ),
        in_specs=[hbm] * 4,
        out_specs=(vmem,) * 4,
        scratch_shapes=[
            pltpu.VMEM((blocks * SLOTS * CH, samples), F32),
            pltpu.VMEM((SLOTS, gene_idx.shape[0]), jnp.int32),
            pltpu.VMEM((CH, genes), F32),
            pltpu.VMEM((samples, blocks * BLOCK), jnp.int32),
            pltpu.VMEM((blocks, BLOCK, SLOTS * CH), BF16),
            pltpu.VMEM((samples, blocks * BLOCK), BF16),
            pltpu.VMEM((CH, genes, samples), F32),
            pltpu.VMEM((CH, genes, samples), F32),
            pltpu.VMEM((CH, rows, samples), F32),
            pltpu.VMEM((2, CH * GSTR, samples), BF16),
            pltpu.VMEM((2, CH * GSTR, samples), BF16),
            pltpu.VMEM((2, CH * GSTR, samples), BF16),
            pltpu.VMEM((2, CH * GSTR, samples), BF16),
            pltpu.VMEM((1, 1, samples), F32),
            pltpu.VMEM((n, 1, samples), F32),
            dma((pieces,)), dma((pieces,)), dma((2,)),
            dma((2,)), dma((2,)), dma((2,)), dma((2,)),
            dma((n,)), dma((n,)),
        ],
        compiler_params=pltpu.CompilerParams(
            collective_id=0, has_side_effects=True, vmem_limit_bytes=24 * 1024 * 1024
        ),
        name="forward",
    )(stay(gene_idx.T), stay(head_weight.T), stay(genotypes), stay(gene_weight))
    grad_w, grad_head, totals = pl.pallas_call(
        backward_kernel,
        out_shape=(
            shape((blocks, BLOCK, SLOTS * CH), F32),
            shape((CH, genes), F32),
            shape((2,), F32),
        ),
        in_specs=[vmem] * 6,
        out_specs=(hbm, hbm, hbm),
        scratch_shapes=[
            pltpu.VMEM((blocks, BLOCK, SLOTS * CH), F32),
            pltpu.VMEM((CH, genes), F32),
            pltpu.SMEM((2,), F32),
            dma((parts,)), dma((2,)),
        ],
        compiler_params=pltpu.CompilerParams(vmem_limit_bytes=24 * 1024 * 1024),
        name="backward",
    )(logit, labels.reshape(1, samples), head_bias.reshape(1, 1), dose, spread, act)
    return (grad_w, grad_head.T, totals)


def solution(mesh):
    placed = (P("grp", "var"), P("grp"), P("var", None, None), P(), P("var", None), P())
    return jax.shard_map(
        per_device,
        mesh=mesh,
        in_specs=placed,
        out_specs=(P(("grp", "var"), None, None), P(("grp", "var"), None), P("grp")),
        check_vma=False,
    )
```

```python
import functools

import jax
import jax.numpy as jnp
from jax import lax
from jax.experimental import pallas as pl
from jax.experimental.pallas import tpu as pltpu
from jax.sharding import PartitionSpec as P

CH = 16
BLOCK = 128
SLOTS = 8
GSTR = 8
CAP = 32
OUT_PARTS = (2, 6, 12, 18, 24, 30)

root_half = 0.7071067811865476
inv_root_tau = 0.3989422804014327

MESH = pl.DeviceIdType.MESH
F32 = jnp.float32
BF16 = jnp.bfloat16
NT = (((1,), (1,)), ((), ()))


def split_blocks(blocks):
    end = CAP // SLOTS
    inner = blocks - 2 * end
    cuts = [end + inner * k // 4 for k in range(5)]
    return [(0, end), (blocks - end, end)] + [(p, q - p) for p, q in zip(cuts, cuts[1:])]


def forward_kernel(
    n, ids_hbm, hw_hbm, geno_hbm, w_hbm,
    dose_ref, turned_ref, act_ref, logit_ref,
    spread_ref, ids_ref, hw_ref, geno, weight, dosage, hs_ref, cdfs, sums, given, taken, lending, lent, share_ref, mine, shares,
    geno_sem, w_sem, small_sem, halo_send, halo_recv, own_send, own_recv, share_send, share_recv,
):
    me = lax.axis_index("var")
    samples = geno.shape[0]
    blocks = weight.shape[0]
    genes = hw_ref.shape[1]
    rows = genes + 2 * GSTR
    edges = blocks * SLOTS
    all_blocks = ids_ref.shape[1]
    edge = 2 * GSTR

    barrier = pltpu.get_barrier_semaphore()

    pieces = split_blocks(blocks)

    def geno_copy(i):
        first, count = pieces[i]
        cols = pl.ds(first * BLOCK, count * BLOCK)
        return pltpu.make_async_copy(geno_hbm.at[:, cols], geno.at[:, cols], geno_sem.at[i])

    def w_copy(i):
        at = pl.ds(*pieces[i])
        return pltpu.make_async_copy(w_hbm.at[at], weight.at[at], w_sem.at[i])

    ids_copy = pltpu.make_async_copy(ids_hbm, ids_ref, small_sem.at[0])
    hw_load = pltpu.make_async_copy(hw_hbm, hw_ref, small_sem.at[1])
    ids_copy.start()
    for i in range(len(pieces)):
        geno_copy(i).start()
        w_copy(i).start()
        if i == 1:
            def greet(j):
                pl.semaphore_signal(
                    barrier, inc=1, device_id={"var": lax.rem(me + j, n)}, device_id_type=MESH
                )

            greet(n - 1)
            greet(1)

            @pl.loop(2, n - 1)
            def _(j):
                greet(j)
    hw_load.start()

    part = spread_ref

    def do_chunk(i):
        geno_copy(i).wait()
        w_copy(i).wait()
        for b in range(pieces[i][0], sum(pieces[i])):
            at = pl.ds(b * BLOCK, BLOCK)
            dose = geno[:, at].astype(F32).astype(BF16)
            dosage[:, at] = dose
            part[at, :] = lax.dot_general(
                weight[b], dose, (((0,), (1,)), ((), ())), preferred_element_type=F32
            )

    ids_copy.wait()
    first = me * genes - GSTR
    ids = ids_ref[...]
    width = -(-all_blocks // 128) * 128
    if width > all_blocks:
        ids = jnp.concatenate([ids, jnp.zeros((SLOTS, width - all_blocks), jnp.int32)], axis=1)
    near = pltpu.roll(ids, lax.rem(width - me * blocks, width), 1)[:, :128] - first
    near = near.astype(F32).astype(BF16)
    chosen = (
        lax.broadcasted_iota(jnp.int32, (edges, 128), 1)
        == lax.broadcasted_iota(jnp.int32, (edges, 128), 0) // SLOTS
    ).astype(F32).astype(BF16)
    wide = lax.dot_general(near, chosen, NT, preferred_element_type=F32)
    slot = lax.broadcasted_iota(jnp.int32, (SLOTS, edges), 0)
    lane = lax.broadcasted_iota(jnp.int32, (SLOTS, edges), 1)
    id_row = jnp.sum(jnp.where(lane % SLOTS == slot, wide, 0.0), axis=0, keepdims=True)
    id_row = id_row.astype(jnp.int32)

    id_ends = jnp.concatenate([id_row[:, :CAP], id_row[:, edges - CAP:]], axis=1)
    id_ends = jnp.concatenate([id_ends, id_ends], axis=1)
    end_at = lax.broadcasted_iota(jnp.int32, (edge, 4 * CAP), 0)
    end_at = jnp.where(end_at < GSTR, end_at, end_at + (rows - edge))
    end_summer = (end_at == id_ends).astype(F32).astype(BF16)

    do_chunk(0)
    do_chunk(1)

    for c in range(0, CH, 2):
        ends = jnp.concatenate([
            jnp.concatenate([
                part[pl.ds(c + k, CAP, stride=CH), :],
                part[pl.ds((edges - CAP) * CH + c + k, CAP, stride=CH), :],
            ], axis=0) for k in range(2)
        ], axis=1)
        high = ends.astype(BF16)
        low = (ends - high.astype(F32)).astype(BF16)
        total = jnp.dot(
            end_summer, jnp.concatenate([high, low], axis=0), preferred_element_type=F32
        )
        for side in range(2):
            these = total[side * GSTR:(side + 1) * GSTR]
            given[side, c * GSTR:(c + 2) * GSTR, :] = jnp.concatenate(
                [these[:, :samples], these[:, samples:]], axis=0
            ).astype(BF16)

    has_lower = me > 0
    has_upper = me < n - 1

    def neighbour(side):
        return {"var": me - 1 if side == 0 else me + 1}

    def halo_copy(side, land):
        return pltpu.make_async_remote_copy(
            src_ref=given.at[side], dst_ref=taken.at[land],
            send_sem=halo_send.at[side], recv_sem=halo_recv.at[land],
            device_id=neighbour(side), device_id_type=MESH,
        )

    def own_copy(side, land):
        return pltpu.make_async_remote_copy(
            src_ref=lending.at[side], dst_ref=lent.at[land],
            send_sem=own_send.at[side], recv_sem=own_recv.at[land],
            device_id=neighbour(side), device_id_type=MESH,
        )

    inner = rows - 2 * edge

    def spread(column, count):
        return jnp.broadcast_to(column, (count, samples))

    def cdf_of(values):
        return 0.5 * (1.0 + lax.erf(values * root_half))

    def slopes_of(values, cdf):
        return cdf + values * jnp.exp(-0.5 * values * values) * inv_root_tau

    def own_work():
        for i in range(2, len(pieces)):
            do_chunk(i)

        gene_at = lax.broadcasted_iota(jnp.int32, (rows, edges), 0)
        summer = (gene_at == id_row).astype(F32).astype(BF16)
        for c in range(0, CH, 2):
            both = jnp.concatenate(
                [part[pl.ds(c, edges, stride=CH), :], part[pl.ds(c + 1, edges, stride=CH), :]], axis=1
            )
            high = both.astype(BF16)
            low = (both - high.astype(F32)).astype(BF16)
            total = jnp.dot(summer, high, preferred_element_type=F32)
            total = total + jnp.dot(summer, low, preferred_element_type=F32)
            sums[c] = total[:, :samples]
            sums[c + 1] = total[:, samples:]
        hw_load.wait()
        hw_own = hw_ref[...].T
        share = jnp.zeros((8, samples), F32)
        for c in range(CH):
            values = sums[c, edge:rows - edge, :]
            cdf = cdf_of(values)
            cdfs[c, GSTR:genes - GSTR, :] = cdf
            hw = spread(hw_own[GSTR:genes - GSTR, c:c + 1], inner)
            share = share + jnp.sum((values * cdf * hw).reshape(inner // 8, 8, samples), axis=0)
        share_ref[...] = share
        for b in range(blocks):
            at = pl.ds(b * BLOCK, BLOCK)
            dose_ref[at, :] = dosage[:, at].T

    ahead = me < n // 8

    @pl.loop(0, 2)
    def _(step):
        @pl.when(step == 1 - ahead.astype(jnp.int32))
        def _():
            own_work()

        @pl.when(step == 0)
        def _():
            pl.semaphore_wait(barrier, n - 1)
            for side, there in ((0, has_lower), (1, has_upper)):
                @pl.when(there)
                def _(side=side):
                    halo_copy(side, 1 - side).start()

                @pl.when(jnp.logical_not(there))
                def _(side=side):
                    taken[side] = jnp.zeros(taken.shape[1:], BF16)
                    lent[side] = jnp.zeros(lent.shape[1:], BF16)

    hw_own = hw_ref[...].T
    share = share_ref[...]

    for side, there in ((0, has_lower), (1, has_upper)):
        @pl.when(there)
        def _(side=side):
            halo_copy(side, side).wait()

    for c in range(CH):
        for side in range(2):
            at = GSTR if side == 0 else rows - edge
            pair = taken[side, c // 2 * 2 * GSTR:(c // 2 + 1) * 2 * GSTR, :].astype(F32)
            values = sums[c, at:at + GSTR, :] + pair[c % 2 * GSTR:(c % 2 + 1) * GSTR]
            cdf = cdf_of(values)
            sums[c, at:at + GSTR, :] = values
            cdfs[c, at - GSTR:at, :] = cdf
            share = share + values * cdf * spread(hw_own[at - GSTR:at, c:c + 1], GSTR)

    mine[0] = jnp.sum(share, axis=0, keepdims=True)

    def share_copy(src, dst, other):
        return pltpu.make_async_remote_copy(
            src_ref=src, dst_ref=dst,
            send_sem=share_send, recv_sem=share_recv,
            device_id={"var": other}, device_id_type=MESH,
        )

    @pl.loop(0, n - 1)
    def _(j):
        other = j + (j >= me).astype(jnp.int32)
        share_copy(mine.at[0], shares.at[me], other).start()

    shares[me] = mine[0]

    for side in range(2):
        at = GSTR if side == 0 else rows - edge
        for c in range(0, CH, 2):
            pair = []
            for k in range(c, c + 2):
                values = sums[k, at:at + GSTR, :]
                hw = spread(hw_own[at - GSTR:at, k:k + 1], GSTR)
                pair.append(hw * slopes_of(values, cdfs[k, at - GSTR:at, :]))
            lending[side, c * GSTR:(c + 2) * GSTR, :] = jnp.concatenate(pair, axis=0).astype(BF16)

    for side, there in ((0, has_lower), (1, has_upper)):
        @pl.when(there)
        def _(side=side):
            own_copy(side, 1 - side).start()

    for c in range(CH):
        values = sums[c, GSTR:rows - GSTR, :]
        cdf = cdfs[c]
        hs_ref[c] = spread(hw_own[:, c:c + 1], genes) * slopes_of(values, cdf)
        act = values * cdf
        high = act.astype(BF16)
        act_ref[c, :samples, :] = high.T
        act_ref[c, samples:, :] = (act - high.astype(F32)).astype(BF16).T

    tall = lax.dot_general(chosen, near, NT, preferred_element_type=F32)
    slot = lax.broadcasted_iota(jnp.int32, (edges, SLOTS), 1)
    sub = lax.broadcasted_iota(jnp.int32, (edges, SLOTS), 0)
    id_col = jnp.sum(jnp.where(sub % SLOTS == slot, tall, 0.0), axis=1, keepdims=True)
    id_col = id_col.astype(jnp.int32)
    gene_at = lax.broadcasted_iota(jnp.int32, (edges, genes), 1) + GSTR
    pick = (gene_at == id_col).astype(F32).astype(BF16)
    id_ends = jnp.concatenate([id_col[:CAP], id_col[edges - CAP:]], axis=0)
    end_at = lax.broadcasted_iota(jnp.int32, (2 * CAP, edge), 1)
    end_at = jnp.where(end_at < GSTR, end_at, end_at + (rows - edge))
    end_pick = (end_at == id_ends).astype(F32).astype(BF16)

    for c in range(0, CH, 2):
        both = jnp.concatenate([hs_ref[c], hs_ref[c + 1]], axis=1)
        high = both.astype(BF16)
        low = (both - high.astype(F32)).astype(BF16)
        picked = jnp.dot(pick, high, preferred_element_type=F32)
        picked = picked + jnp.dot(pick, low, preferred_element_type=F32)
        spread_ref[pl.ds(c, edges, stride=CH), :] = picked[:, :samples]
        spread_ref[pl.ds(c + 1, edges, stride=CH), :] = picked[:, samples:]

    def turn(b):
        at = pl.ds(b * BLOCK, BLOCK)
        turned_ref[b] = spread_ref[at, :].T

    for b in range(CAP // SLOTS, blocks - CAP // SLOTS):
        turn(b)

    for side, there in ((0, has_lower), (1, has_upper)):
        @pl.when(there)
        def _(side=side):
            own_copy(side, side).wait()

    for c in range(0, CH, 2):
        sides = []
        for side in range(2):
            pair = lent[side, c * GSTR:(c + 2) * GSTR, :].astype(F32)
            sides.append(jnp.concatenate([pair[:GSTR], pair[GSTR:]], axis=1))
        both = jnp.concatenate(sides, axis=0).astype(BF16)
        picked = jnp.dot(end_pick, both, preferred_element_type=F32)
        for k in range(2):
            cols = slice(k * samples, (k + 1) * samples)
            for side in range(2):
                at = pl.ds(side * (edges - CAP) * CH + c + k, CAP, stride=CH)
                spread_ref[at, :] = spread_ref[at, :] + picked[side * CAP:(side + 1) * CAP, cols]

    for b in range(CAP // SLOTS):
        turn(b)
        turn(blocks - 1 - b)

    arrived = shares.at[pl.ds(0, n - 1)]
    share_copy(arrived, arrived, lax.rem(me + 1, n)).wait()

    logit_ref[...] = jnp.sum(shares[...], axis=0)


def backward_kernel(
    logit_ref, labels_ref, bias_ref, dose_ref, spread_ref, act_ref,
    grad_w_hbm, grad_head_hbm, totals_hbm, out, head, totals, out_sem, small_sem,
):
    samples = dose_ref.shape[1]
    blocks = out.shape[0]
    logits = logit_ref[...] + bias_ref[0]
    targets = labels_ref[...].astype(F32)
    dlogit = jax.nn.sigmoid(logits) - targets
    tall = jnp.broadcast_to(dlogit, (samples, samples)).T
    cuts = [blocks * p // OUT_PARTS[-1] for p in (0,) + OUT_PARTS]

    def out_copy(i):
        at = pl.ds(cuts[i], cuts[i + 1] - cuts[i])
        return pltpu.make_async_copy(out.at[at], grad_w_hbm.at[at], out_sem.at[i])

    for i in range(len(OUT_PARTS)):
        for b in range(cuts[i], cuts[i + 1]):
            grad_gene = (tall * spread_ref[b]).astype(BF16)
            out[b] = jnp.dot(
                dose_ref[pl.ds(b * BLOCK, BLOCK), :], grad_gene, preferred_element_type=F32
            )
        out_copy(i).start()

    loss = jnp.maximum(logits, 0.0) + jnp.log1p(jnp.exp(-jnp.abs(logits))) - targets * logits
    totals[0] = jnp.sum(loss)
    totals[1] = jnp.sum(dlogit)
    totals_copy = pltpu.make_async_copy(totals, totals_hbm, small_sem.at[0])
    totals_copy.start()

    top = dlogit.astype(BF16).astype(F32)
    middle = (dlogit - top).astype(BF16).astype(F32)
    rest = dlogit - top - middle
    row = lax.broadcasted_iota(jnp.int32, (8, samples), 0)
    parts = jnp.where(row == 0, top, jnp.where(row == 1, middle, jnp.where(row == 2, rest, 0.0)))
    parts = jnp.concatenate([parts, parts], axis=1).astype(BF16)
    for c in range(CH):
        found = jnp.dot(parts, act_ref[c], preferred_element_type=F32)
        head[c:c + 1, :] = jnp.sum(found, axis=0, keepdims=True)
    head_copy = pltpu.make_async_copy(head, grad_head_hbm, small_sem.at[1])
    head_copy.start()
    for i in range(len(OUT_PARTS)):
        out_copy(i).wait()
    totals_copy.wait()
    head_copy.wait()


def per_device(genotypes, labels, gene_weight, gene_idx, head_weight, head_bias):
    samples = genotypes.shape[0]
    blocks = gene_weight.shape[0]
    genes = head_weight.shape[0]
    rows = genes + 2 * GSTR
    n = lax.axis_size("var")
    vmem = pl.BlockSpec(memory_space=pltpu.VMEM)
    hbm = pl.BlockSpec(memory_space=pltpu.HBM)
    smem = pl.BlockSpec(memory_space=pltpu.SMEM)
    shape = jax.ShapeDtypeStruct
    dma = pltpu.SemaphoreType.DMA
    pieces = len(split_blocks(blocks))
    parts = len(OUT_PARTS)
    stay = functools.partial(pltpu.with_memory_space_constraint, memory_space=pltpu.HBM)
    dose, spread, act, logit = pl.pallas_call(
        functools.partial(forward_kernel, n),
        out_shape=(
            shape((blocks * BLOCK, samples), BF16),
            shape((blocks, samples, SLOTS * CH), F32),
            shape((CH, 2 * samples, genes), BF16),
            shape((1, samples), F32),
        ),
        in_specs=[hbm] * 4,
        out_specs=(vmem,) * 4,
        scratch_shapes=[
            pltpu.VMEM((blocks * SLOTS * CH, samples), F32),
            pltpu.VMEM((SLOTS, gene_idx.shape[0]), jnp.int32),
            pltpu.VMEM((CH, genes), F32),
            pltpu.VMEM((samples, blocks * BLOCK), jnp.int32),
            pltpu.VMEM((blocks, BLOCK, SLOTS * CH), BF16),
            pltpu.VMEM((samples, blocks * BLOCK), BF16),
            pltpu.VMEM((CH, genes, samples), F32),
            pltpu.VMEM((CH, genes, samples), F32),
            pltpu.VMEM((CH, rows, samples), F32),
            pltpu.VMEM((2, CH * GSTR, samples), BF16),
            pltpu.VMEM((2, CH * GSTR, samples), BF16),
            pltpu.VMEM((2, CH * GSTR, samples), BF16),
            pltpu.VMEM((2, CH * GSTR, samples), BF16),
            pltpu.VMEM((8, samples), F32),
            pltpu.VMEM((1, 1, samples), F32),
            pltpu.VMEM((n, 1, samples), F32),
            dma((pieces,)), dma((pieces,)), dma((2,)),
            dma((2,)), dma((2,)), dma((2,)), dma((2,)),
            dma, dma,
        ],
        compiler_params=pltpu.CompilerParams(
            collective_id=0, has_side_effects=True, vmem_limit_bytes=24 * 1024 * 1024
        ),
        name="forward",
    )(stay(gene_idx.T), stay(head_weight.T), stay(genotypes), stay(gene_weight))
    grad_w, grad_head, totals = pl.pallas_call(
        backward_kernel,
        out_shape=(
            shape((blocks, BLOCK, SLOTS * CH), F32),
            shape((CH, genes), F32),
            shape((2,), F32),
        ),
        in_specs=[vmem, vmem, smem, vmem, vmem, vmem],
        out_specs=(hbm, hbm, hbm),
        scratch_shapes=[
            pltpu.VMEM((blocks, BLOCK, SLOTS * CH), F32),
            pltpu.VMEM((CH, genes), F32),
            pltpu.SMEM((2,), F32),
            dma((parts,)), dma((2,)),
        ],
        compiler_params=pltpu.CompilerParams(vmem_limit_bytes=24 * 1024 * 1024),
        name="backward",
    )(logit, labels.reshape(1, samples), head_bias, dose, spread, act)
    return (grad_w, grad_head.T, totals)


def solution(mesh):
    placed = (P("grp", "var"), P("grp"), P("var", None, None), P(), P("var", None), P())
    return jax.shard_map(
        per_device,
        mesh=mesh,
        in_specs=placed,
        out_specs=(P(("grp", "var"), None, None), P(("grp", "var"), None), P("grp")),
        check_vma=False,
    )
```

```python
import functools

import jax
import jax.numpy as jnp
from jax import lax
from jax.experimental import pallas as pl
from jax.experimental.pallas import tpu as pltpu
from jax.sharding import PartitionSpec as P

CH = 16
BLOCK = 128
SLOTS = 8
GSTR = 8
CAP = 32
OUT_PARTS = (2, 6, 12, 18, 24, 30)

root_half = 0.7071067811865476
inv_root_tau = 0.3989422804014327

MESH = pl.DeviceIdType.MESH
F32 = jnp.float32
BF16 = jnp.bfloat16
NT = (((1,), (1,)), ((), ()))


def split_blocks(blocks):
    end = CAP // SLOTS
    inner = blocks - 2 * end
    cuts = [end + inner * k // 4 for k in range(5)]
    return [(0, end), (blocks - end, end)] + [(p, q - p) for p, q in zip(cuts, cuts[1:])]


def forward_kernel(
    n, ids_hbm, hw_hbm, geno_hbm, w_hbm,
    dose_ref, turned_ref, act_ref, logit_ref,
    spread_ref, ids_ref, hw_ref, geno, weight, dosage, hs_ref, cdfs, sums, given, taken, lending, lent, share_ref, mine, shares,
    geno_sem, w_sem, small_sem, halo_send, halo_recv, own_send, own_recv, share_send, share_recv,
):
    me = lax.axis_index("var")
    samples = geno.shape[0]
    blocks = weight.shape[0]
    genes = hw_ref.shape[1]
    rows = genes + 2 * GSTR
    edges = blocks * SLOTS
    all_blocks = ids_ref.shape[1]
    edge = 2 * GSTR

    barrier = pltpu.get_barrier_semaphore()

    pieces = split_blocks(blocks)

    def geno_copy(i):
        first, count = pieces[i]
        cols = pl.ds(first * BLOCK, count * BLOCK)
        return pltpu.make_async_copy(geno_hbm.at[:, cols], geno.at[:, cols], geno_sem.at[i])

    def w_copy(i):
        at = pl.ds(*pieces[i])
        return pltpu.make_async_copy(w_hbm.at[at], weight.at[at], w_sem.at[i])

    ids_copy = pltpu.make_async_copy(ids_hbm, ids_ref, small_sem.at[0])
    hw_load = pltpu.make_async_copy(hw_hbm, hw_ref, small_sem.at[1])
    ids_copy.start()
    for i in range(len(pieces)):
        geno_copy(i).start()
        w_copy(i).start()
        if i == 1:
            def greet(j):
                pl.semaphore_signal(
                    barrier, inc=1, device_id={"var": lax.rem(me + j, n)}, device_id_type=MESH
                )

            greet(n - 1)
            greet(1)

            @pl.loop(2, n - 1)
            def _(j):
                greet(j)
    hw_load.start()

    part = spread_ref

    def wait_chunk(i):
        geno_copy(i).wait()
        w_copy(i).wait()

    def do_chunk(i):
        for b in range(pieces[i][0], sum(pieces[i])):
            at = pl.ds(b * BLOCK, BLOCK)
            dose = geno[:, at].astype(F32).astype(BF16)
            dosage[:, at] = dose
            part[at, :] = lax.dot_general(
                weight[b], dose, (((0,), (1,)), ((), ())), preferred_element_type=F32
            )

    ids_copy.wait()
    wait_chunk(0)
    wait_chunk(1)
    first = me * genes - GSTR
    ids = ids_ref[...]
    width = -(-all_blocks // 128) * 128
    if width > all_blocks:
        ids = jnp.concatenate([ids, jnp.zeros((SLOTS, width - all_blocks), jnp.int32)], axis=1)
    near = pltpu.roll(ids, lax.rem(width - me * blocks, width), 1)[:, :128] - first
    near = near.astype(F32).astype(BF16)
    chosen = (
        lax.broadcasted_iota(jnp.int32, (edges, 128), 1)
        == lax.broadcasted_iota(jnp.int32, (edges, 128), 0) // SLOTS
    ).astype(F32).astype(BF16)
    wide = lax.dot_general(near, chosen, NT, preferred_element_type=F32)
    slot = lax.broadcasted_iota(jnp.int32, (SLOTS, edges), 0)
    lane = lax.broadcasted_iota(jnp.int32, (SLOTS, edges), 1)
    id_row = jnp.sum(jnp.where(lane % SLOTS == slot, wide, 0.0), axis=0, keepdims=True)
    id_row = id_row.astype(jnp.int32)

    id_ends = jnp.concatenate([id_row[:, :CAP], id_row[:, edges - CAP:]], axis=1)
    id_ends = jnp.concatenate([id_ends, id_ends], axis=1)
    end_at = lax.broadcasted_iota(jnp.int32, (edge, 4 * CAP), 0)
    end_at = jnp.where(end_at < GSTR, end_at, end_at + (rows - edge))
    end_summer = (end_at == id_ends).astype(F32).astype(BF16)

    do_chunk(0)
    do_chunk(1)

    for c in range(0, CH, 2):
        ends = jnp.concatenate([
            jnp.concatenate([
                part[pl.ds(c + k, CAP, stride=CH), :],
                part[pl.ds((edges - CAP) * CH + c + k, CAP, stride=CH), :],
            ], axis=0) for k in range(2)
        ], axis=1)
        high = ends.astype(BF16)
        low = (ends - high.astype(F32)).astype(BF16)
        total = jnp.dot(
            end_summer, jnp.concatenate([high, low], axis=0), preferred_element_type=F32
        )
        for side in range(2):
            these = total[side * GSTR:(side + 1) * GSTR]
            given[side, c * GSTR:(c + 2) * GSTR, :] = jnp.concatenate(
                [these[:, :samples], these[:, samples:]], axis=0
            ).astype(BF16)

    has_lower = me > 0
    has_upper = me < n - 1

    def neighbour(side):
        return {"var": me - 1 if side == 0 else me + 1}

    def halo_copy(side, land):
        return pltpu.make_async_remote_copy(
            src_ref=given.at[side], dst_ref=taken.at[land],
            send_sem=halo_send.at[side], recv_sem=halo_recv.at[land],
            device_id=neighbour(side), device_id_type=MESH,
        )

    def own_copy(side, land):
        return pltpu.make_async_remote_copy(
            src_ref=lending.at[side], dst_ref=lent.at[land],
            send_sem=own_send.at[side], recv_sem=own_recv.at[land],
            device_id=neighbour(side), device_id_type=MESH,
        )

    inner = rows - 2 * edge

    def spread(column, count):
        return jnp.broadcast_to(column, (count, samples))

    def cdf_of(values):
        return 0.5 * (1.0 + lax.erf(values * root_half))

    def slopes_of(values, cdf):
        return cdf + values * jnp.exp(-0.5 * values * values) * inv_root_tau

    def own_work():
        for i in range(2, len(pieces)):
            wait_chunk(i)
            do_chunk(i)

        gene_at = lax.broadcasted_iota(jnp.int32, (rows, edges), 0)
        summer = (gene_at == id_row).astype(F32).astype(BF16)
        for c in range(0, CH, 2):
            both = jnp.concatenate(
                [part[pl.ds(c, edges, stride=CH), :], part[pl.ds(c + 1, edges, stride=CH), :]], axis=1
            )
            high = both.astype(BF16)
            low = (both - high.astype(F32)).astype(BF16)
            total = jnp.dot(summer, high, preferred_element_type=F32)
            total = total + jnp.dot(summer, low, preferred_element_type=F32)
            sums[c] = total[:, :samples]
            sums[c + 1] = total[:, samples:]
        hw_load.wait()
        hw_own = hw_ref[...].T
        share = jnp.zeros((8, samples), F32)
        for c in range(CH):
            values = sums[c, edge:rows - edge, :]
            cdf = cdf_of(values)
            cdfs[c, GSTR:genes - GSTR, :] = cdf
            hw = spread(hw_own[GSTR:genes - GSTR, c:c + 1], inner)
            share = share + jnp.sum((values * cdf * hw).reshape(inner // 8, 8, samples), axis=0)
        share_ref[...] = share

    def turn_dosage():
        for b in range(blocks):
            at = pl.ds(b * BLOCK, BLOCK)
            dose_ref[at, :] = dosage[:, at].T

    ahead = me < n // 8


    @pl.loop(0, 2)
    def _(step):
        @pl.when(step == 1 - ahead.astype(jnp.int32))
        def _():
            own_work()

            @pl.when(ahead)
            def _():
                turn_dosage()

        @pl.when(step == 0)
        def _():
            pl.semaphore_wait(barrier, n - 1)
            for side, there in ((0, has_lower), (1, has_upper)):
                @pl.when(there)
                def _(side=side):
                    halo_copy(side, 1 - side).start()

                @pl.when(jnp.logical_not(there))
                def _(side=side):
                    taken[side] = jnp.zeros(taken.shape[1:], BF16)
                    lent[side] = jnp.zeros(lent.shape[1:], BF16)

    hw_own = hw_ref[...].T
    share = share_ref[...]

    for side, there in ((0, has_lower), (1, has_upper)):
        @pl.when(there)
        def _(side=side):
            halo_copy(side, side).wait()

    for c in range(CH):
        for side in range(2):
            at = GSTR if side == 0 else rows - edge
            pair = taken[side, c // 2 * 2 * GSTR:(c // 2 + 1) * 2 * GSTR, :].astype(F32)
            values = sums[c, at:at + GSTR, :] + pair[c % 2 * GSTR:(c % 2 + 1) * GSTR]
            cdf = cdf_of(values)
            sums[c, at:at + GSTR, :] = values
            cdfs[c, at - GSTR:at, :] = cdf
            share = share + values * cdf * spread(hw_own[at - GSTR:at, c:c + 1], GSTR)

    mine[0] = jnp.sum(share, axis=0, keepdims=True)

    def share_copy(src, dst, other):
        return pltpu.make_async_remote_copy(
            src_ref=src, dst_ref=dst,
            send_sem=share_send, recv_sem=share_recv,
            device_id={"var": other}, device_id_type=MESH,
        )

    @pl.loop(0, n - 1)
    def _(j):
        other = j + (j >= me).astype(jnp.int32)
        share_copy(mine.at[0], shares.at[me], other).start()

    shares[me] = mine[0]

    for side in range(2):
        at = GSTR if side == 0 else rows - edge
        for c in range(0, CH, 2):
            pair = []
            for k in range(c, c + 2):
                values = sums[k, at:at + GSTR, :]
                hw = spread(hw_own[at - GSTR:at, k:k + 1], GSTR)
                pair.append(hw * slopes_of(values, cdfs[k, at - GSTR:at, :]))
            lending[side, c * GSTR:(c + 2) * GSTR, :] = jnp.concatenate(pair, axis=0).astype(BF16)

    for side, there in ((0, has_lower), (1, has_upper)):
        @pl.when(there)
        def _(side=side):
            own_copy(side, 1 - side).start()

    for c in range(CH):
        values = sums[c, GSTR:rows - GSTR, :]
        cdf = cdfs[c]
        hs_ref[c] = spread(hw_own[:, c:c + 1], genes) * slopes_of(values, cdf)
        act = values * cdf
        high = act.astype(BF16)
        act_ref[c, :samples, :] = high.T
        act_ref[c, samples:, :] = (act - high.astype(F32)).astype(BF16).T

    @pl.when(jnp.logical_not(ahead))
    def _():
        turn_dosage()

    tall = lax.dot_general(chosen, near, NT, preferred_element_type=F32)
    slot = lax.broadcasted_iota(jnp.int32, (edges, SLOTS), 1)
    sub = lax.broadcasted_iota(jnp.int32, (edges, SLOTS), 0)
    id_col = jnp.sum(jnp.where(sub % SLOTS == slot, tall, 0.0), axis=1, keepdims=True)
    id_col = id_col.astype(jnp.int32)
    gene_at = lax.broadcasted_iota(jnp.int32, (edges, genes), 1) + GSTR
    pick = (gene_at == id_col).astype(F32).astype(BF16)
    id_ends = jnp.concatenate([id_col[:CAP], id_col[edges - CAP:]], axis=0)
    end_at = lax.broadcasted_iota(jnp.int32, (2 * CAP, edge), 1)
    end_at = jnp.where(end_at < GSTR, end_at, end_at + (rows - edge))
    end_pick = (end_at == id_ends).astype(F32).astype(BF16)

    for c in range(0, CH, 2):
        both = jnp.concatenate([hs_ref[c], hs_ref[c + 1]], axis=1)
        high = both.astype(BF16)
        low = (both - high.astype(F32)).astype(BF16)
        picked = jnp.dot(pick, high, preferred_element_type=F32)
        picked = picked + jnp.dot(pick, low, preferred_element_type=F32)
        spread_ref[pl.ds(c, edges, stride=CH), :] = picked[:, :samples]
        spread_ref[pl.ds(c + 1, edges, stride=CH), :] = picked[:, samples:]

    def turn(b):
        at = pl.ds(b * BLOCK, BLOCK)
        turned_ref[b] = spread_ref[at, :].T

    for b in range(CAP // SLOTS, blocks - CAP // SLOTS):
        turn(b)

    for side, there in ((0, has_lower), (1, has_upper)):
        @pl.when(there)
        def _(side=side):
            own_copy(side, side).wait()

    for c in range(0, CH, 2):
        sides = []
        for side in range(2):
            pair = lent[side, c * GSTR:(c + 2) * GSTR, :].astype(F32)
            sides.append(jnp.concatenate([pair[:GSTR], pair[GSTR:]], axis=1))
        both = jnp.concatenate(sides, axis=0).astype(BF16)
        picked = jnp.dot(end_pick, both, preferred_element_type=F32)
        for k in range(2):
            cols = slice(k * samples, (k + 1) * samples)
            for side in range(2):
                at = pl.ds(side * (edges - CAP) * CH + c + k, CAP, stride=CH)
                spread_ref[at, :] = spread_ref[at, :] + picked[side * CAP:(side + 1) * CAP, cols]

    for b in range(CAP // SLOTS):
        turn(b)
        turn(blocks - 1 - b)

    arrived = shares.at[pl.ds(0, n - 1)]
    share_copy(arrived, arrived, lax.rem(me + 1, n)).wait()

    logit_ref[...] = jnp.sum(shares[...], axis=0)


def backward_kernel(
    logit_ref, labels_ref, bias_ref, dose_ref, spread_ref, act_ref,
    grad_w_hbm, grad_head_hbm, totals_hbm, out, head, totals, out_sem, small_sem,
):
    samples = dose_ref.shape[1]
    blocks = out.shape[0]
    logits = logit_ref[...] + bias_ref[0]
    targets = labels_ref[...].astype(F32)
    dlogit = jax.nn.sigmoid(logits) - targets
    tall = jnp.broadcast_to(dlogit, (samples, samples)).T
    cuts = [blocks * p // OUT_PARTS[-1] for p in (0,) + OUT_PARTS]

    def out_copy(i):
        at = pl.ds(cuts[i], cuts[i + 1] - cuts[i])
        return pltpu.make_async_copy(out.at[at], grad_w_hbm.at[at], out_sem.at[i])

    for i in range(len(OUT_PARTS)):
        for b in range(cuts[i], cuts[i + 1]):
            grad_gene = (tall * spread_ref[b]).astype(BF16)
            out[b] = jnp.dot(
                dose_ref[pl.ds(b * BLOCK, BLOCK), :], grad_gene, preferred_element_type=F32
            )
        out_copy(i).start()

    loss = jnp.maximum(logits, 0.0) + jnp.log1p(jnp.exp(-jnp.abs(logits))) - targets * logits
    totals[0] = jnp.sum(loss)
    totals[1] = jnp.sum(dlogit)
    totals_copy = pltpu.make_async_copy(totals, totals_hbm, small_sem.at[0])
    totals_copy.start()

    top = dlogit.astype(BF16).astype(F32)
    middle = (dlogit - top).astype(BF16).astype(F32)
    rest = dlogit - top - middle
    row = lax.broadcasted_iota(jnp.int32, (8, samples), 0)
    parts = jnp.where(row == 0, top, jnp.where(row == 1, middle, jnp.where(row == 2, rest, 0.0)))
    parts = jnp.concatenate([parts, parts], axis=1).astype(BF16)
    for c in range(CH):
        found = jnp.dot(parts, act_ref[c], preferred_element_type=F32)
        head[c:c + 1, :] = jnp.sum(found, axis=0, keepdims=True)
    head_copy = pltpu.make_async_copy(head, grad_head_hbm, small_sem.at[1])
    head_copy.start()
    for i in range(len(OUT_PARTS)):
        out_copy(i).wait()
    totals_copy.wait()
    head_copy.wait()


def per_device(genotypes, labels, gene_weight, gene_idx, head_weight, head_bias):
    samples = genotypes.shape[0]
    blocks = gene_weight.shape[0]
    genes = head_weight.shape[0]
    rows = genes + 2 * GSTR
    n = lax.axis_size("var")
    vmem = pl.BlockSpec(memory_space=pltpu.VMEM)
    hbm = pl.BlockSpec(memory_space=pltpu.HBM)
    smem = pl.BlockSpec(memory_space=pltpu.SMEM)
    shape = jax.ShapeDtypeStruct
    dma = pltpu.SemaphoreType.DMA
    pieces = len(split_blocks(blocks))
    parts = len(OUT_PARTS)
    stay = functools.partial(pltpu.with_memory_space_constraint, memory_space=pltpu.HBM)
    dose, spread, act, logit = pl.pallas_call(
        functools.partial(forward_kernel, n),
        out_shape=(
            shape((blocks * BLOCK, samples), BF16),
            shape((blocks, samples, SLOTS * CH), F32),
            shape((CH, 2 * samples, genes), BF16),
            shape((1, samples), F32),
        ),
        in_specs=[hbm] * 4,
        out_specs=(vmem,) * 4,
        scratch_shapes=[
            pltpu.VMEM((blocks * SLOTS * CH, samples), F32),
            pltpu.VMEM((SLOTS, gene_idx.shape[0]), jnp.int32),
            pltpu.VMEM((CH, genes), F32),
            pltpu.VMEM((samples, blocks * BLOCK), jnp.int32),
            pltpu.VMEM((blocks, BLOCK, SLOTS * CH), BF16),
            pltpu.VMEM((samples, blocks * BLOCK), BF16),
            pltpu.VMEM((CH, genes, samples), F32),
            pltpu.VMEM((CH, genes, samples), F32),
            pltpu.VMEM((CH, rows, samples), F32),
            pltpu.VMEM((2, CH * GSTR, samples), BF16),
            pltpu.VMEM((2, CH * GSTR, samples), BF16),
            pltpu.VMEM((2, CH * GSTR, samples), BF16),
            pltpu.VMEM((2, CH * GSTR, samples), BF16),
            pltpu.VMEM((8, samples), F32),
            pltpu.VMEM((1, 1, samples), F32),
            pltpu.VMEM((n, 1, samples), F32),
            dma((pieces,)), dma((pieces,)), dma((2,)),
            dma((2,)), dma((2,)), dma((2,)), dma((2,)),
            dma, dma,
        ],
        compiler_params=pltpu.CompilerParams(
            collective_id=0, has_side_effects=True, vmem_limit_bytes=24 * 1024 * 1024
        ),
        name="forward",
    )(stay(gene_idx.T), stay(head_weight.T), stay(genotypes), stay(gene_weight))
    grad_w, grad_head, totals = pl.pallas_call(
        backward_kernel,
        out_shape=(
            shape((blocks, BLOCK, SLOTS * CH), F32),
            shape((CH, genes), F32),
            shape((2,), F32),
        ),
        in_specs=[vmem, vmem, smem, vmem, vmem, vmem],
        out_specs=(hbm, hbm, hbm),
        scratch_shapes=[
            pltpu.VMEM((blocks, BLOCK, SLOTS * CH), F32),
            pltpu.VMEM((CH, genes), F32),
            pltpu.SMEM((2,), F32),
            dma((parts,)), dma((2,)),
        ],
        compiler_params=pltpu.CompilerParams(vmem_limit_bytes=24 * 1024 * 1024),
        name="backward",
    )(logit, labels.reshape(1, samples), head_bias, dose, spread, act)
    return (grad_w, grad_head.T, totals)


def solution(mesh):
    placed = (P("grp", "var"), P("grp"), P("var", None, None), P(), P("var", None), P())
    return jax.shard_map(
        per_device,
        mesh=mesh,
        in_specs=placed,
        out_specs=(P(("grp", "var"), None, None), P(("grp", "var"), None), P("grp")),
        check_vma=False,
    )
```

```python
import functools

import jax
import jax.numpy as jnp
from jax import lax
from jax.experimental import pallas as pl
from jax.experimental.pallas import tpu as pltpu
from jax.sharding import PartitionSpec as P

CH = 16
BLOCK = 128
SLOTS = 8
GSTR = 8
CAP = 32
OUT_PARTS = (2, 6, 12, 18, 24, 30)

root_half = 0.7071067811865476
inv_root_tau = 0.3989422804014327

MESH = pl.DeviceIdType.MESH
F32 = jnp.float32
BF16 = jnp.bfloat16
NT = (((1,), (1,)), ((), ()))


def split_blocks(blocks):
    end = CAP // SLOTS
    inner = blocks - 2 * end
    cuts = [end + inner * k // 4 for k in range(5)]
    return [(0, end), (blocks - end, end)] + [(p, q - p) for p, q in zip(cuts, cuts[1:])]


def forward_kernel(
    n, ids_hbm, hw_hbm, geno_hbm, w_hbm,
    dose_ref, turned_ref, act_ref, logit_ref,
    spread_ref, ids_ref, hw_ref, geno, weight, dosage, hs_ref, cdfs, sums, given, taken, lending, lent, hw_wide, share_ref, mine, shares,
    geno_sem, w_sem, small_sem, halo_send, halo_recv, own_send, own_recv, share_send, share_recv,
):
    me = lax.axis_index("var")
    samples = geno.shape[0]
    blocks = weight.shape[0]
    genes = hw_ref.shape[1]
    rows = genes + 2 * GSTR
    edges = blocks * SLOTS
    all_blocks = ids_ref.shape[1]
    edge = 2 * GSTR

    barrier = pltpu.get_barrier_semaphore()

    pieces = split_blocks(blocks)

    def geno_copy(i):
        first, count = pieces[i]
        cols = pl.ds(first * BLOCK, count * BLOCK)
        return pltpu.make_async_copy(geno_hbm.at[:, cols], geno.at[:, cols], geno_sem.at[i])

    def w_copy(i):
        at = pl.ds(*pieces[i])
        return pltpu.make_async_copy(w_hbm.at[at], weight.at[at], w_sem.at[i])

    ids_copy = pltpu.make_async_copy(ids_hbm, ids_ref, small_sem.at[0])
    hw_load = pltpu.make_async_copy(hw_hbm, hw_ref, small_sem.at[1])
    ids_copy.start()
    hw_load.start()
    for i in range(len(pieces)):
        geno_copy(i).start()
        w_copy(i).start()
        if i == 1:
            def greet(j):
                pl.semaphore_signal(
                    barrier, inc=1, device_id={"var": lax.rem(me + j, n)}, device_id_type=MESH
                )

            greet(n - 1)
            greet(1)

            @pl.loop(2, n - 1)
            def _(j):
                greet(j)


    def wait_chunk(i):
        geno_copy(i).wait()
        w_copy(i).wait()

    def do_chunk(i):
        for b in range(pieces[i][0], sum(pieces[i])):
            at = pl.ds(b * BLOCK, BLOCK)
            dose = geno[:, at].astype(F32).astype(BF16)
            dosage[:, at] = dose
            found = lax.dot_general(
                weight[b], dose, (((0,), (1,)), ((), ())), preferred_element_type=F32
            )
            found = jnp.swapaxes(found.reshape(SLOTS, CH, samples), 0, 1)
            spread_ref[:, pl.ds(b * SLOTS, SLOTS), :] = found

    hw_load.wait()
    hw_own = hw_ref[...].T
    for c in range(CH):
        hw_wide[c] = jnp.broadcast_to(hw_own[:, c:c + 1], (genes, samples))
    ids_copy.wait()
    wait_chunk(0)
    wait_chunk(1)
    first = me * genes - GSTR
    ids = ids_ref[...]
    width = -(-all_blocks // 128) * 128
    if width > all_blocks:
        ids = jnp.concatenate([ids, jnp.zeros((SLOTS, width - all_blocks), jnp.int32)], axis=1)
    near = pltpu.roll(ids, lax.rem(width - me * blocks, width), 1)[:, :128] - first
    near = near.astype(F32).astype(BF16)
    chosen = (
        lax.broadcasted_iota(jnp.int32, (edges, 128), 1)
        == lax.broadcasted_iota(jnp.int32, (edges, 128), 0) // SLOTS
    ).astype(F32).astype(BF16)
    wide = lax.dot_general(near, chosen, NT, preferred_element_type=F32)
    slot = lax.broadcasted_iota(jnp.int32, (SLOTS, edges), 0)
    lane = lax.broadcasted_iota(jnp.int32, (SLOTS, edges), 1)
    id_row = jnp.sum(jnp.where(lane % SLOTS == slot, wide, 0.0), axis=0, keepdims=True)
    id_row = id_row.astype(jnp.int32)

    id_ends = jnp.concatenate([id_row[:, :CAP], id_row[:, edges - CAP:]], axis=1)
    id_ends = jnp.concatenate([id_ends, id_ends], axis=1)
    end_at = lax.broadcasted_iota(jnp.int32, (edge, 4 * CAP), 0)
    end_at = jnp.where(end_at < GSTR, end_at, end_at + (rows - edge))
    end_summer = (end_at == id_ends).astype(F32).astype(BF16)

    do_chunk(0)
    do_chunk(1)

    for c in range(0, CH, 2):
        ends = jnp.concatenate([
            jnp.concatenate([
                spread_ref[c + k, :CAP, :], spread_ref[c + k, edges - CAP:, :],
            ], axis=0) for k in range(2)
        ], axis=1)
        high = ends.astype(BF16)
        low = (ends - high.astype(F32)).astype(BF16)
        total = jnp.dot(
            end_summer, jnp.concatenate([high, low], axis=0), preferred_element_type=F32
        )
        for side in range(2):
            these = total[side * GSTR:(side + 1) * GSTR]
            given[side, c * GSTR:(c + 2) * GSTR, :] = jnp.concatenate(
                [these[:, :samples], these[:, samples:]], axis=0
            ).astype(BF16)

    has_lower = me > 0
    has_upper = me < n - 1

    def neighbour(side):
        return {"var": me - 1 if side == 0 else me + 1}

    def halo_copy(side, land):
        return pltpu.make_async_remote_copy(
            src_ref=given.at[side], dst_ref=taken.at[land],
            send_sem=halo_send.at[side], recv_sem=halo_recv.at[land],
            device_id=neighbour(side), device_id_type=MESH,
        )

    def own_copy(side, land):
        return pltpu.make_async_remote_copy(
            src_ref=lending.at[side], dst_ref=lent.at[land],
            send_sem=own_send.at[side], recv_sem=own_recv.at[land],
            device_id=neighbour(side), device_id_type=MESH,
        )

    inner = rows - 2 * edge

    def cdf_of(values):
        return 0.5 * (1.0 + lax.erf(values * root_half))

    def slopes_of(values, cdf):
        return cdf + values * jnp.exp(-0.5 * values * values) * inv_root_tau

    def own_work():
        for i in range(2, len(pieces)):
            wait_chunk(i)
            do_chunk(i)

        gene_at = lax.broadcasted_iota(jnp.int32, (rows, edges), 0)
        summer = (gene_at == id_row).astype(F32).astype(BF16)
        for c in range(0, CH, 2):
            both = jnp.concatenate(
                [spread_ref[c], spread_ref[c + 1]], axis=1
            )
            high = both.astype(BF16)
            low = (both - high.astype(F32)).astype(BF16)
            total = jnp.dot(summer, high, preferred_element_type=F32)
            total = total + jnp.dot(summer, low, preferred_element_type=F32)
            sums[c] = total[:, :samples]
            sums[c + 1] = total[:, samples:]
        share = jnp.zeros((8, samples), F32)
        for c in range(CH):
            values = sums[c, edge:rows - edge, :]
            cdf = cdf_of(values)
            cdfs[c, GSTR:genes - GSTR, :] = cdf
            hw = hw_wide[c, GSTR:genes - GSTR, :]
            share = share + jnp.sum((values * cdf * hw).reshape(inner // 8, 8, samples), axis=0)
        share_ref[...] = share

    def turn_dosage():
        for b in range(blocks):
            at = pl.ds(b * BLOCK, BLOCK)
            dose_ref[at, :] = dosage[:, at].T

    ahead = me < n // 8


    @pl.loop(0, 2)
    def _(step):
        @pl.when(step == 1 - ahead.astype(jnp.int32))
        def _():
            own_work()

            @pl.when(ahead)
            def _():
                turn_dosage()

        @pl.when(step == 0)
        def _():
            pl.semaphore_wait(barrier, n - 1)
            for side, there in ((0, has_lower), (1, has_upper)):
                @pl.when(there)
                def _(side=side):
                    halo_copy(side, 1 - side).start()

                @pl.when(jnp.logical_not(there))
                def _(side=side):
                    taken[side] = jnp.zeros(taken.shape[1:], BF16)
                    lent[side] = jnp.zeros(lent.shape[1:], BF16)

    share = share_ref[...]

    for side, there in ((0, has_lower), (1, has_upper)):
        @pl.when(there)
        def _(side=side):
            halo_copy(side, side).wait()

    for c in range(CH):
        for side in range(2):
            at = GSTR if side == 0 else rows - edge
            pair = taken[side, c // 2 * 2 * GSTR:(c // 2 + 1) * 2 * GSTR, :].astype(F32)
            values = sums[c, at:at + GSTR, :] + pair[c % 2 * GSTR:(c % 2 + 1) * GSTR]
            cdf = cdf_of(values)
            sums[c, at:at + GSTR, :] = values
            cdfs[c, at - GSTR:at, :] = cdf
            share = share + values * cdf * hw_wide[c, at - GSTR:at, :]

    mine[0] = jnp.sum(share, axis=0, keepdims=True)

    def share_copy(src, dst, other):
        return pltpu.make_async_remote_copy(
            src_ref=src, dst_ref=dst,
            send_sem=share_send, recv_sem=share_recv,
            device_id={"var": other}, device_id_type=MESH,
        )

    @pl.loop(0, n - 1)
    def _(j):
        other = j + (j >= me).astype(jnp.int32)
        share_copy(mine.at[0], shares.at[me], other).start()

    shares[me] = mine[0]

    for side in range(2):
        at = GSTR if side == 0 else rows - edge
        for c in range(0, CH, 2):
            pair = []
            for k in range(c, c + 2):
                values = sums[k, at:at + GSTR, :]
                hw = hw_wide[k, at - GSTR:at, :]
                pair.append(hw * slopes_of(values, cdfs[k, at - GSTR:at, :]))
            lending[side, c * GSTR:(c + 2) * GSTR, :] = jnp.concatenate(pair, axis=0).astype(BF16)

    for side, there in ((0, has_lower), (1, has_upper)):
        @pl.when(there)
        def _(side=side):
            own_copy(side, 1 - side).start()

    for c in range(CH):
        values = sums[c, GSTR:rows - GSTR, :]
        cdf = cdfs[c]
        hs_ref[c] = hw_wide[c] * slopes_of(values, cdf)
        act = values * cdf
        high = act.astype(BF16)
        act_ref[c, :samples, :] = high.T
        act_ref[c, samples:, :] = (act - high.astype(F32)).astype(BF16).T

    @pl.when(jnp.logical_not(ahead))
    def _():
        turn_dosage()

    tall = lax.dot_general(chosen, near, NT, preferred_element_type=F32)
    slot = lax.broadcasted_iota(jnp.int32, (edges, SLOTS), 1)
    sub = lax.broadcasted_iota(jnp.int32, (edges, SLOTS), 0)
    id_col = jnp.sum(jnp.where(sub % SLOTS == slot, tall, 0.0), axis=1, keepdims=True)
    id_col = id_col.astype(jnp.int32)
    gene_at = lax.broadcasted_iota(jnp.int32, (edges, genes), 1) + GSTR
    pick = (gene_at == id_col).astype(F32).astype(BF16)
    id_ends = jnp.concatenate([id_col[:CAP], id_col[edges - CAP:]], axis=0)
    end_at = lax.broadcasted_iota(jnp.int32, (2 * CAP, edge), 1)
    end_at = jnp.where(end_at < GSTR, end_at, end_at + (rows - edge))
    end_pick = (end_at == id_ends).astype(F32).astype(BF16)

    for c in range(0, CH, 2):
        both = jnp.concatenate([hs_ref[c], hs_ref[c + 1]], axis=1)
        high = both.astype(BF16)
        low = (both - high.astype(F32)).astype(BF16)
        picked = jnp.dot(pick, high, preferred_element_type=F32)
        picked = picked + jnp.dot(pick, low, preferred_element_type=F32)
        spread_ref[c] = picked[:, :samples]
        spread_ref[c + 1] = picked[:, samples:]

    def turn(b):
        these = jnp.swapaxes(spread_ref[:, pl.ds(b * SLOTS, SLOTS), :], 0, 1)
        turned_ref[b] = these.reshape(SLOTS * CH, samples).T

    for b in range(CAP // SLOTS, blocks - CAP // SLOTS):
        turn(b)

    for side, there in ((0, has_lower), (1, has_upper)):
        @pl.when(there)
        def _(side=side):
            own_copy(side, side).wait()

    for c in range(0, CH, 2):
        sides = []
        for side in range(2):
            pair = lent[side, c * GSTR:(c + 2) * GSTR, :].astype(F32)
            sides.append(jnp.concatenate([pair[:GSTR], pair[GSTR:]], axis=1))
        both = jnp.concatenate(sides, axis=0).astype(BF16)
        picked = jnp.dot(end_pick, both, preferred_element_type=F32)
        for k in range(2):
            cols = slice(k * samples, (k + 1) * samples)
            for side in range(2):
                at = pl.ds(side * (edges - CAP), CAP)
                spread_ref[c + k, at, :] = (
                    spread_ref[c + k, at, :] + picked[side * CAP:(side + 1) * CAP, cols]
                )

    for b in range(CAP // SLOTS):
        turn(b)
        turn(blocks - 1 - b)

    arrived = shares.at[pl.ds(0, n - 1)]
    share_copy(arrived, arrived, lax.rem(me + 1, n)).wait()

    logit_ref[...] = jnp.sum(shares[...], axis=0)


def backward_kernel(
    logit_ref, labels_ref, bias_ref, dose_ref, spread_ref, act_ref,
    grad_w_hbm, grad_head_hbm, totals_hbm, out, head, totals, out_sem, small_sem,
):
    samples = dose_ref.shape[1]
    blocks = out.shape[0]
    logits = logit_ref[...] + bias_ref[0]
    targets = labels_ref[...].astype(F32)
    dlogit = jax.nn.sigmoid(logits) - targets
    tall = jnp.broadcast_to(dlogit, (samples, samples)).T
    cuts = [blocks * p // OUT_PARTS[-1] for p in (0,) + OUT_PARTS]

    def out_copy(i):
        at = pl.ds(cuts[i], cuts[i + 1] - cuts[i])
        return pltpu.make_async_copy(out.at[at], grad_w_hbm.at[at], out_sem.at[i])

    for i in range(len(OUT_PARTS)):
        for b in range(cuts[i], cuts[i + 1]):
            grad_gene = (tall * spread_ref[b]).astype(BF16)
            out[b] = jnp.dot(
                dose_ref[pl.ds(b * BLOCK, BLOCK), :], grad_gene, preferred_element_type=F32
            )
        out_copy(i).start()

    loss = jnp.maximum(logits, 0.0) + jnp.log1p(jnp.exp(-jnp.abs(logits))) - targets * logits
    totals[0] = jnp.sum(loss)
    totals[1] = jnp.sum(dlogit)
    totals_copy = pltpu.make_async_copy(totals, totals_hbm, small_sem.at[0])
    totals_copy.start()

    top = dlogit.astype(BF16).astype(F32)
    middle = (dlogit - top).astype(BF16).astype(F32)
    rest = dlogit - top - middle
    row = lax.broadcasted_iota(jnp.int32, (8, samples), 0)
    parts = jnp.where(row == 0, top, jnp.where(row == 1, middle, jnp.where(row == 2, rest, 0.0)))
    parts = jnp.concatenate([parts, parts], axis=1).astype(BF16)
    for c in range(CH):
        found = jnp.dot(parts, act_ref[c], preferred_element_type=F32)
        head[c:c + 1, :] = jnp.sum(found, axis=0, keepdims=True)
    head_copy = pltpu.make_async_copy(head, grad_head_hbm, small_sem.at[1])
    head_copy.start()
    for i in range(len(OUT_PARTS)):
        out_copy(i).wait()
    totals_copy.wait()
    head_copy.wait()


def per_device(genotypes, labels, gene_weight, gene_idx, head_weight, head_bias):
    samples = genotypes.shape[0]
    blocks = gene_weight.shape[0]
    genes = head_weight.shape[0]
    rows = genes + 2 * GSTR
    n = lax.axis_size("var")
    vmem = pl.BlockSpec(memory_space=pltpu.VMEM)
    hbm = pl.BlockSpec(memory_space=pltpu.HBM)
    smem = pl.BlockSpec(memory_space=pltpu.SMEM)
    shape = jax.ShapeDtypeStruct
    dma = pltpu.SemaphoreType.DMA
    pieces = len(split_blocks(blocks))
    parts = len(OUT_PARTS)
    stay = functools.partial(pltpu.with_memory_space_constraint, memory_space=pltpu.HBM)
    dose, spread, act, logit = pl.pallas_call(
        functools.partial(forward_kernel, n),
        out_shape=(
            shape((blocks * BLOCK, samples), BF16),
            shape((blocks, samples, SLOTS * CH), F32),
            shape((CH, 2 * samples, genes), BF16),
            shape((1, samples), F32),
        ),
        in_specs=[hbm] * 4,
        out_specs=(vmem,) * 4,
        scratch_shapes=[
            pltpu.VMEM((CH, blocks * SLOTS, samples), F32),
            pltpu.VMEM((SLOTS, gene_idx.shape[0]), jnp.int32),
            pltpu.VMEM((CH, genes), F32),
            pltpu.VMEM((samples, blocks * BLOCK), jnp.int32),
            pltpu.VMEM((blocks, BLOCK, SLOTS * CH), BF16),
            pltpu.VMEM((samples, blocks * BLOCK), BF16),
            pltpu.VMEM((CH, genes, samples), F32),
            pltpu.VMEM((CH, genes, samples), F32),
            pltpu.VMEM((CH, rows, samples), F32),
            pltpu.VMEM((2, CH * GSTR, samples), BF16),
            pltpu.VMEM((2, CH * GSTR, samples), BF16),
            pltpu.VMEM((2, CH * GSTR, samples), BF16),
            pltpu.VMEM((2, CH * GSTR, samples), BF16),
            pltpu.VMEM((CH, genes, samples), F32),
            pltpu.VMEM((8, samples), F32),
            pltpu.VMEM((1, 1, samples), F32),
            pltpu.VMEM((n, 1, samples), F32),
            dma((pieces,)), dma((pieces,)), dma((2,)),
            dma((2,)), dma((2,)), dma((2,)), dma((2,)),
            dma, dma,
        ],
        compiler_params=pltpu.CompilerParams(
            collective_id=0, has_side_effects=True, vmem_limit_bytes=24 * 1024 * 1024
        ),
        name="forward",
    )(stay(gene_idx.T), stay(head_weight.T), stay(genotypes), stay(gene_weight))
    grad_w, grad_head, totals = pl.pallas_call(
        backward_kernel,
        out_shape=(
            shape((blocks, BLOCK, SLOTS * CH), F32),
            shape((CH, genes), F32),
            shape((2,), F32),
        ),
        in_specs=[vmem, vmem, smem, vmem, vmem, vmem],
        out_specs=(hbm, hbm, hbm),
        scratch_shapes=[
            pltpu.VMEM((blocks, BLOCK, SLOTS * CH), F32),
            pltpu.VMEM((CH, genes), F32),
            pltpu.SMEM((2,), F32),
            dma((parts,)), dma((2,)),
        ],
        compiler_params=pltpu.CompilerParams(vmem_limit_bytes=24 * 1024 * 1024),
        name="backward",
    )(logit, labels.reshape(1, samples), head_bias, dose, spread, act)
    return (grad_w, grad_head.T, totals)


def solution(mesh):
    placed = (P("grp", "var"), P("grp"), P("var", None, None), P(), P("var", None), P())
    return jax.shard_map(
        per_device,
        mesh=mesh,
        in_specs=placed,
        out_specs=(P(("grp", "var"), None, None), P(("grp", "var"), None), P("grp")),
        check_vma=False,
    )
```

```python
import functools

import jax
import jax.numpy as jnp
from jax import lax
from jax.experimental import pallas as pl
from jax.experimental.pallas import tpu as pltpu
from jax.sharding import PartitionSpec as P

CH = 16
BLOCK = 128
SLOTS = 8
GSTR = 8
CAP = 32
OUT_PARTS = (2, 6, 12, 18, 24, 30)

root_half = 0.7071067811865476
inv_root_tau = 0.3989422804014327

MESH = pl.DeviceIdType.MESH
F32 = jnp.float32
BF16 = jnp.bfloat16
NT = (((1,), (1,)), ((), ()))


def split_blocks(blocks):
    end = CAP // SLOTS
    inner = blocks - 2 * end
    cuts = [end + inner * k // 2 for k in range(3)]
    return [(0, end), (blocks - end, end)] + [(p, q - p) for p, q in zip(cuts, cuts[1:])]


def forward_kernel(
    n, ids_hbm, hw_hbm, geno_hbm, w_hbm,
    dose_ref, turned_ref, act_ref, logit_ref,
    spread_ref, ids_ref, hw_ref, geno, weight, dosage, hs_ref, cdfs, sums, given, taken, lending, lent, hw_wide, share_ref, mine, shares,
    geno_sem, w_sem, small_sem, halo_send, halo_recv, own_send, own_recv, share_send, share_recv,
):
    me = lax.axis_index("var")
    samples = geno.shape[0]
    blocks = weight.shape[0]
    genes = hw_ref.shape[1]
    rows = genes + 2 * GSTR
    edges = blocks * SLOTS
    all_blocks = ids_ref.shape[1]
    edge = 2 * GSTR

    barrier = pltpu.get_barrier_semaphore()

    pieces = split_blocks(blocks)

    def geno_copy(i):
        first, count = pieces[i]
        cols = pl.ds(first * BLOCK, count * BLOCK)
        return pltpu.make_async_copy(geno_hbm.at[:, cols], geno.at[:, cols], geno_sem.at[i])

    def w_copy(i):
        at = pl.ds(*pieces[i])
        return pltpu.make_async_copy(w_hbm.at[at], weight.at[at], w_sem.at[i])

    ids_copy = pltpu.make_async_copy(ids_hbm, ids_ref, small_sem.at[0])
    hw_load = pltpu.make_async_copy(hw_hbm, hw_ref, small_sem.at[1])
    ids_copy.start()
    hw_load.start()
    for i in range(len(pieces)):
        geno_copy(i).start()
        w_copy(i).start()
        if i == 0:
            def greet(j):
                pl.semaphore_signal(
                    barrier, inc=1, device_id={"var": lax.rem(me + j, n)}, device_id_type=MESH
                )

            greet(n - 1)
            greet(1)

            @pl.loop(2, n - 1)
            def _(j):
                greet(j)


    def wait_chunk(i):
        geno_copy(i).wait()
        w_copy(i).wait()

    def do_chunk(i):
        for b in range(pieces[i][0], sum(pieces[i])):
            at = pl.ds(b * BLOCK, BLOCK)
            dose = geno[:, at].astype(F32).astype(BF16)
            dosage[:, at] = dose
            found = lax.dot_general(
                weight[b], dose, (((0,), (1,)), ((), ())), preferred_element_type=F32
            )
            found = jnp.swapaxes(found.reshape(SLOTS, CH, samples), 0, 1)
            spread_ref[:, pl.ds(b * SLOTS, SLOTS), :] = found

    hw_load.wait()
    hw_own = hw_ref[...].T
    for c in range(CH):
        hw_wide[c] = jnp.broadcast_to(hw_own[:, c:c + 1], (genes, samples))
    ids_copy.wait()
    wait_chunk(0)
    wait_chunk(1)
    first = me * genes - GSTR
    ids = ids_ref[...]
    width = -(-all_blocks // 128) * 128
    if width > all_blocks:
        ids = jnp.concatenate([ids, jnp.zeros((SLOTS, width - all_blocks), jnp.int32)], axis=1)
    near = pltpu.roll(ids, lax.rem(width - me * blocks, width), 1)[:, :128] - first
    near = near.astype(F32).astype(BF16)
    chosen = (
        lax.broadcasted_iota(jnp.int32, (edges, 128), 1)
        == lax.broadcasted_iota(jnp.int32, (edges, 128), 0) // SLOTS
    ).astype(F32).astype(BF16)
    wide = lax.dot_general(near, chosen, NT, preferred_element_type=F32)
    slot = lax.broadcasted_iota(jnp.int32, (SLOTS, edges), 0)
    lane = lax.broadcasted_iota(jnp.int32, (SLOTS, edges), 1)
    id_row = jnp.sum(jnp.where(lane % SLOTS == slot, wide, 0.0), axis=0, keepdims=True)
    id_row = id_row.astype(jnp.int32)

    id_ends = jnp.concatenate([id_row[:, :CAP], id_row[:, edges - CAP:]], axis=1)
    id_ends = jnp.concatenate([id_ends, id_ends], axis=1)
    end_at = lax.broadcasted_iota(jnp.int32, (edge, 4 * CAP), 0)
    end_at = jnp.where(end_at < GSTR, end_at, end_at + (rows - edge))
    end_summer = (end_at == id_ends).astype(F32).astype(BF16)

    do_chunk(0)
    do_chunk(1)

    for c in range(0, CH, 2):
        ends = jnp.concatenate([
            jnp.concatenate([
                spread_ref[c + k, :CAP, :], spread_ref[c + k, edges - CAP:, :],
            ], axis=0) for k in range(2)
        ], axis=1)
        high = ends.astype(BF16)
        low = (ends - high.astype(F32)).astype(BF16)
        total = jnp.dot(
            end_summer, jnp.concatenate([high, low], axis=0), preferred_element_type=F32
        )
        for side in range(2):
            these = total[side * GSTR:(side + 1) * GSTR]
            given[side, c * GSTR:(c + 2) * GSTR, :] = jnp.concatenate(
                [these[:, :samples], these[:, samples:]], axis=0
            ).astype(BF16)

    has_lower = me > 0
    has_upper = me < n - 1

    def neighbour(side):
        return {"var": me - 1 if side == 0 else me + 1}

    def halo_copy(side, land):
        return pltpu.make_async_remote_copy(
            src_ref=given.at[side], dst_ref=taken.at[land],
            send_sem=halo_send.at[side], recv_sem=halo_recv.at[land],
            device_id=neighbour(side), device_id_type=MESH,
        )

    def own_copy(side, land):
        return pltpu.make_async_remote_copy(
            src_ref=lending.at[side], dst_ref=lent.at[land],
            send_sem=own_send.at[side], recv_sem=own_recv.at[land],
            device_id=neighbour(side), device_id_type=MESH,
        )

    inner = rows - 2 * edge

    def cdf_of(values):
        return 0.5 * (1.0 + lax.erf(values * root_half))

    def slopes_of(values, cdf):
        return cdf + values * jnp.exp(-0.5 * values * values) * inv_root_tau

    def own_work():
        for i in range(2, len(pieces)):
            wait_chunk(i)
            do_chunk(i)

        gene_at = lax.broadcasted_iota(jnp.int32, (rows, edges), 0)
        summer = (gene_at == id_row).astype(F32).astype(BF16)
        for c in range(0, CH, 2):
            both = jnp.concatenate(
                [spread_ref[c], spread_ref[c + 1]], axis=1
            )
            high = both.astype(BF16)
            low = (both - high.astype(F32)).astype(BF16)
            total = jnp.dot(summer, high, preferred_element_type=F32)
            total = total + jnp.dot(summer, low, preferred_element_type=F32)
            sums[c] = total[:, :samples]
            sums[c + 1] = total[:, samples:]
        share = jnp.zeros((8, samples), F32)
        for c in range(CH):
            values = sums[c, edge:rows - edge, :]
            cdf = cdf_of(values)
            cdfs[c, GSTR:genes - GSTR, :] = cdf
            hw = hw_wide[c, GSTR:genes - GSTR, :]
            share = share + jnp.sum((values * cdf * hw).reshape(inner // 8, 8, samples), axis=0)
        share_ref[...] = share

    def turn_dosage():
        for b in range(blocks):
            at = pl.ds(b * BLOCK, BLOCK)
            dose_ref[at, :] = dosage[:, at].T

    ahead = me < n // 8


    @pl.loop(0, 2)
    def _(step):
        @pl.when(step == 1 - ahead.astype(jnp.int32))
        def _():
            own_work()

            @pl.when(ahead)
            def _():
                turn_dosage()

        @pl.when(step == 0)
        def _():
            pl.semaphore_wait(barrier, n - 1)
            for side, there in ((0, has_lower), (1, has_upper)):
                @pl.when(there)
                def _(side=side):
                    halo_copy(side, 1 - side).start()

                @pl.when(jnp.logical_not(there))
                def _(side=side):
                    taken[side] = jnp.zeros(taken.shape[1:], BF16)
                    lent[side] = jnp.zeros(lent.shape[1:], BF16)

    share = share_ref[...]

    for side, there in ((0, has_lower), (1, has_upper)):
        @pl.when(there)
        def _(side=side):
            halo_copy(side, side).wait()

    for c in range(CH):
        for side in range(2):
            at = GSTR if side == 0 else rows - edge
            pair = taken[side, c // 2 * 2 * GSTR:(c // 2 + 1) * 2 * GSTR, :].astype(F32)
            values = sums[c, at:at + GSTR, :] + pair[c % 2 * GSTR:(c % 2 + 1) * GSTR]
            cdf = cdf_of(values)
            sums[c, at:at + GSTR, :] = values
            cdfs[c, at - GSTR:at, :] = cdf
            share = share + values * cdf * hw_wide[c, at - GSTR:at, :]

    mine[0] = jnp.sum(share, axis=0, keepdims=True)

    def share_copy(src, dst, other):
        return pltpu.make_async_remote_copy(
            src_ref=src, dst_ref=dst,
            send_sem=share_send, recv_sem=share_recv,
            device_id={"var": other}, device_id_type=MESH,
        )

    @pl.loop(0, n - 1)
    def _(j):
        other = j + (j >= me).astype(jnp.int32)
        share_copy(mine.at[0], shares.at[me], other).start()

    shares[me] = mine[0]

    for side in range(2):
        at = GSTR if side == 0 else rows - edge
        for c in range(0, CH, 2):
            pair = []
            for k in range(c, c + 2):
                values = sums[k, at:at + GSTR, :]
                hw = hw_wide[k, at - GSTR:at, :]
                pair.append(hw * slopes_of(values, cdfs[k, at - GSTR:at, :]))
            lending[side, c * GSTR:(c + 2) * GSTR, :] = jnp.concatenate(pair, axis=0).astype(BF16)

    for side, there in ((0, has_lower), (1, has_upper)):
        @pl.when(there)
        def _(side=side):
            own_copy(side, 1 - side).start()

    for c in range(CH):
        values = sums[c, GSTR:rows - GSTR, :]
        cdf = cdfs[c]
        hs_ref[c] = hw_wide[c] * slopes_of(values, cdf)
        act = values * cdf
        high = act.astype(BF16)
        act_ref[c, :samples, :] = high.T
        act_ref[c, samples:, :] = (act - high.astype(F32)).astype(BF16).T

    @pl.when(jnp.logical_not(ahead))
    def _():
        turn_dosage()

    tall = lax.dot_general(chosen, near, NT, preferred_element_type=F32)
    slot = lax.broadcasted_iota(jnp.int32, (edges, SLOTS), 1)
    sub = lax.broadcasted_iota(jnp.int32, (edges, SLOTS), 0)
    id_col = jnp.sum(jnp.where(sub % SLOTS == slot, tall, 0.0), axis=1, keepdims=True)
    id_col = id_col.astype(jnp.int32)
    gene_at = lax.broadcasted_iota(jnp.int32, (edges, genes), 1) + GSTR
    pick = (gene_at == id_col).astype(F32).astype(BF16)
    id_ends = jnp.concatenate([id_col[:CAP], id_col[edges - CAP:]], axis=0)
    end_at = lax.broadcasted_iota(jnp.int32, (2 * CAP, edge), 1)
    end_at = jnp.where(end_at < GSTR, end_at, end_at + (rows - edge))
    end_pick = (end_at == id_ends).astype(F32).astype(BF16)

    for c in range(0, CH, 2):
        both = jnp.concatenate([hs_ref[c], hs_ref[c + 1]], axis=1)
        high = both.astype(BF16)
        low = (both - high.astype(F32)).astype(BF16)
        picked = jnp.dot(pick, high, preferred_element_type=F32)
        picked = picked + jnp.dot(pick, low, preferred_element_type=F32)
        spread_ref[c] = picked[:, :samples]
        spread_ref[c + 1] = picked[:, samples:]

    def turn(b):
        these = jnp.swapaxes(spread_ref[:, pl.ds(b * SLOTS, SLOTS), :], 0, 1)
        turned_ref[b] = these.reshape(SLOTS * CH, samples).T

    for b in range(CAP // SLOTS, blocks - CAP // SLOTS):
        turn(b)

    for side, there in ((0, has_lower), (1, has_upper)):
        @pl.when(there)
        def _(side=side):
            own_copy(side, side).wait()

    for c in range(0, CH, 2):
        sides = []
        for side in range(2):
            pair = lent[side, c * GSTR:(c + 2) * GSTR, :].astype(F32)
            sides.append(jnp.concatenate([pair[:GSTR], pair[GSTR:]], axis=1))
        both = jnp.concatenate(sides, axis=0).astype(BF16)
        picked = jnp.dot(end_pick, both, preferred_element_type=F32)
        for k in range(2):
            cols = slice(k * samples, (k + 1) * samples)
            for side in range(2):
                at = pl.ds(side * (edges - CAP), CAP)
                spread_ref[c + k, at, :] = (
                    spread_ref[c + k, at, :] + picked[side * CAP:(side + 1) * CAP, cols]
                )

    for b in range(CAP // SLOTS):
        turn(b)
        turn(blocks - 1 - b)

    arrived = shares.at[pl.ds(0, n - 1)]
    share_copy(arrived, arrived, lax.rem(me + 1, n)).wait()

    logit_ref[...] = jnp.sum(shares[...], axis=0)


def backward_kernel(
    logit_ref, labels_ref, bias_ref, dose_ref, spread_ref, act_ref,
    grad_w_hbm, grad_head_hbm, totals_hbm, out, head, totals, out_sem, small_sem,
):
    samples = dose_ref.shape[1]
    blocks = out.shape[0]
    logits = logit_ref[...] + bias_ref[0]
    targets = labels_ref[...].astype(F32)
    dlogit = jax.nn.sigmoid(logits) - targets
    tall = jnp.broadcast_to(dlogit, (samples, samples)).T
    cuts = [blocks * p // OUT_PARTS[-1] for p in (0,) + OUT_PARTS]

    def out_copy(i):
        at = pl.ds(cuts[i], cuts[i + 1] - cuts[i])
        return pltpu.make_async_copy(out.at[at], grad_w_hbm.at[at], out_sem.at[i])

    for i in range(len(OUT_PARTS)):
        for b in range(cuts[i], cuts[i + 1]):
            grad_gene = (tall * spread_ref[b]).astype(BF16)
            out[b] = jnp.dot(
                dose_ref[pl.ds(b * BLOCK, BLOCK), :], grad_gene, preferred_element_type=F32
            )
        out_copy(i).start()

    loss = jnp.maximum(logits, 0.0) + jnp.log1p(jnp.exp(-jnp.abs(logits))) - targets * logits
    totals[0] = jnp.sum(loss)
    totals[1] = jnp.sum(dlogit)
    totals_copy = pltpu.make_async_copy(totals, totals_hbm, small_sem.at[0])
    totals_copy.start()

    top = dlogit.astype(BF16).astype(F32)
    middle = (dlogit - top).astype(BF16).astype(F32)
    rest = dlogit - top - middle
    row = lax.broadcasted_iota(jnp.int32, (8, samples), 0)
    parts = jnp.where(row == 0, top, jnp.where(row == 1, middle, jnp.where(row == 2, rest, 0.0)))
    parts = jnp.concatenate([parts, parts], axis=1).astype(BF16)
    for c in range(CH):
        found = jnp.dot(parts, act_ref[c], preferred_element_type=F32)
        head[c:c + 1, :] = jnp.sum(found, axis=0, keepdims=True)
    head_copy = pltpu.make_async_copy(head, grad_head_hbm, small_sem.at[1])
    head_copy.start()
    for i in range(len(OUT_PARTS)):
        out_copy(i).wait()
    totals_copy.wait()
    head_copy.wait()


def per_device(genotypes, labels, gene_weight, gene_idx, head_weight, head_bias):
    samples = genotypes.shape[0]
    blocks = gene_weight.shape[0]
    genes = head_weight.shape[0]
    rows = genes + 2 * GSTR
    n = lax.axis_size("var")
    vmem = pl.BlockSpec(memory_space=pltpu.VMEM)
    hbm = pl.BlockSpec(memory_space=pltpu.HBM)
    smem = pl.BlockSpec(memory_space=pltpu.SMEM)
    shape = jax.ShapeDtypeStruct
    dma = pltpu.SemaphoreType.DMA
    pieces = len(split_blocks(blocks))
    parts = len(OUT_PARTS)
    stay = functools.partial(pltpu.with_memory_space_constraint, memory_space=pltpu.HBM)
    dose, spread, act, logit = pl.pallas_call(
        functools.partial(forward_kernel, n),
        out_shape=(
            shape((blocks * BLOCK, samples), BF16),
            shape((blocks, samples, SLOTS * CH), F32),
            shape((CH, 2 * samples, genes), BF16),
            shape((1, samples), F32),
        ),
        in_specs=[hbm] * 4,
        out_specs=(vmem,) * 4,
        scratch_shapes=[
            pltpu.VMEM((CH, blocks * SLOTS, samples), F32),
            pltpu.VMEM((SLOTS, gene_idx.shape[0]), jnp.int32),
            pltpu.VMEM((CH, genes), F32),
            pltpu.VMEM((samples, blocks * BLOCK), jnp.int32),
            pltpu.VMEM((blocks, BLOCK, SLOTS * CH), BF16),
            pltpu.VMEM((samples, blocks * BLOCK), BF16),
            pltpu.VMEM((CH, genes, samples), F32),
            pltpu.VMEM((CH, genes, samples), F32),
            pltpu.VMEM((CH, rows, samples), F32),
            pltpu.VMEM((2, CH * GSTR, samples), BF16),
            pltpu.VMEM((2, CH * GSTR, samples), BF16),
            pltpu.VMEM((2, CH * GSTR, samples), BF16),
            pltpu.VMEM((2, CH * GSTR, samples), BF16),
            pltpu.VMEM((CH, genes, samples), F32),
            pltpu.VMEM((8, samples), F32),
            pltpu.VMEM((1, 1, samples), F32),
            pltpu.VMEM((n, 1, samples), F32),
            dma((pieces,)), dma((pieces,)), dma((2,)),
            dma((2,)), dma((2,)), dma((2,)), dma((2,)),
            dma, dma,
        ],
        compiler_params=pltpu.CompilerParams(
            collective_id=0, has_side_effects=True, vmem_limit_bytes=24 * 1024 * 1024
        ),
        name="forward",
    )(stay(gene_idx.T), stay(head_weight.T), stay(genotypes), stay(gene_weight))
    grad_w, grad_head, totals = pl.pallas_call(
        backward_kernel,
        out_shape=(
            shape((blocks, BLOCK, SLOTS * CH), F32),
            shape((CH, genes), F32),
            shape((2,), F32),
        ),
        in_specs=[vmem, vmem, smem, vmem, vmem, vmem],
        out_specs=(hbm, hbm, hbm),
        scratch_shapes=[
            pltpu.VMEM((blocks, BLOCK, SLOTS * CH), F32),
            pltpu.VMEM((CH, genes), F32),
            pltpu.SMEM((2,), F32),
            dma((parts,)), dma((2,)),
        ],
        compiler_params=pltpu.CompilerParams(vmem_limit_bytes=24 * 1024 * 1024),
        name="backward",
    )(logit, labels.reshape(1, samples), head_bias, dose, spread, act)
    return (grad_w, grad_head.T, totals)


def solution(mesh):
    placed = (P("grp", "var"), P("grp"), P("var", None, None), P(), P("var", None), P())
    return jax.shard_map(
        per_device,
        mesh=mesh,
        in_specs=placed,
        out_specs=(P(("grp", "var"), None, None), P(("grp", "var"), None), P("grp")),
        check_vma=False,
    )
```

```python
import functools

import jax
import jax.numpy as jnp
from jax import lax
from jax.experimental import pallas as pl
from jax.experimental.pallas import tpu as pltpu
from jax.sharding import PartitionSpec as P

CH = 16
BLOCK = 128
SLOTS = 8
GSTR = 8
CAP = 32
OUT_PARTS = (2, 6, 12, 18, 24, 30)

root_half = 0.7071067811865476
inv_root_tau = 0.3989422804014327

MESH = pl.DeviceIdType.MESH
F32 = jnp.float32
BF16 = jnp.bfloat16
NT = (((1,), (1,)), ((), ()))


def split_blocks(blocks):
    end = CAP // SLOTS
    inner = blocks - 2 * end
    cuts = [end + inner * k // 2 for k in range(3)]
    return [(0, end), (blocks - end, end)] + [(p, q - p) for p, q in zip(cuts, cuts[1:])]


def forward_kernel(
    n, ids_hbm, hw_hbm, geno_hbm, w_hbm,
    dose_ref, turned_ref, act_ref, logit_ref,
    spread_ref, ids_ref, hw_ref, geno, weight, dosage, hs_ref, cdfs, sums, given, taken, lending, lent, hw_wide, share_ref, mine, shares,
    geno_sem, w_sem, small_sem, halo_send, halo_recv, own_send, own_recv, share_send, share_recv,
):
    me = lax.axis_index("var")
    samples = geno.shape[0]
    blocks = weight.shape[0]
    genes = hw_ref.shape[1]
    rows = genes + 2 * GSTR
    edges = blocks * SLOTS
    all_blocks = ids_ref.shape[1]
    edge = 2 * GSTR

    barrier = pltpu.get_barrier_semaphore()

    pieces = split_blocks(blocks)

    def geno_copy(i):
        first, count = pieces[i]
        cols = pl.ds(first * BLOCK, count * BLOCK)
        return pltpu.make_async_copy(geno_hbm.at[:, cols], geno.at[:, cols], geno_sem.at[i])

    def w_copy(i):
        at = pl.ds(*pieces[i])
        return pltpu.make_async_copy(w_hbm.at[at], weight.at[at], w_sem.at[i])

    ids_copy = pltpu.make_async_copy(ids_hbm, ids_ref, small_sem.at[0])
    hw_load = pltpu.make_async_copy(hw_hbm, hw_ref, small_sem.at[1])
    ids_copy.start()
    hw_load.start()
    for i in range(len(pieces)):
        geno_copy(i).start()
        w_copy(i).start()
        if i == 0:
            def greet(j):
                pl.semaphore_signal(
                    barrier, inc=1, device_id={"var": lax.rem(me + j, n)}, device_id_type=MESH
                )

            greet(n - 1)
            greet(1)

            @pl.loop(2, n - 1)
            def _(j):
                greet(j)


    def wait_chunk(i):
        geno_copy(i).wait()
        w_copy(i).wait()

    def do_chunk(i):
        for b in range(pieces[i][0], sum(pieces[i])):
            at = pl.ds(b * BLOCK, BLOCK)
            dose = geno[:, at].astype(F32).astype(BF16)
            dosage[:, at] = dose
            found = lax.dot_general(
                weight[b], dose, (((0,), (1,)), ((), ())), preferred_element_type=F32
            )
            found = jnp.swapaxes(found.reshape(SLOTS, CH, samples), 0, 1)
            spread_ref[:, pl.ds(b * SLOTS, SLOTS), :] = found

    hw_load.wait()
    hw_own = hw_ref[...].T
    for c in range(CH):
        hw_wide[c] = jnp.broadcast_to(hw_own[:, c:c + 1], (genes, samples))
    ids_copy.wait()
    wait_chunk(0)
    wait_chunk(1)
    first = me * genes - GSTR
    ids = ids_ref[...]
    width = -(-all_blocks // 128) * 128
    if width > all_blocks:
        ids = jnp.concatenate([ids, jnp.zeros((SLOTS, width - all_blocks), jnp.int32)], axis=1)
    near = pltpu.roll(ids, lax.rem(width - me * blocks, width), 1)[:, :128] - first
    near = near.astype(F32).astype(BF16)
    chosen = (
        lax.broadcasted_iota(jnp.int32, (edges, 128), 1)
        == lax.broadcasted_iota(jnp.int32, (edges, 128), 0) // SLOTS
    ).astype(F32).astype(BF16)
    wide = lax.dot_general(near, chosen, NT, preferred_element_type=F32)
    slot = lax.broadcasted_iota(jnp.int32, (SLOTS, edges), 0)
    lane = lax.broadcasted_iota(jnp.int32, (SLOTS, edges), 1)
    id_row = jnp.sum(jnp.where(lane % SLOTS == slot, wide, 0.0), axis=0, keepdims=True)
    id_row = id_row.astype(jnp.int32)

    id_ends = jnp.concatenate([id_row[:, :CAP], id_row[:, edges - CAP:]], axis=1)
    id_ends = jnp.concatenate([id_ends, id_ends], axis=1)
    end_at = lax.broadcasted_iota(jnp.int32, (edge, 4 * CAP), 0)
    end_at = jnp.where(end_at < GSTR, end_at, end_at + (rows - edge))
    end_summer = (end_at == id_ends).astype(F32).astype(BF16)

    do_chunk(0)
    do_chunk(1)

    for c in range(0, CH, 2):
        ends = jnp.concatenate([
            jnp.concatenate([
                spread_ref[c + k, :CAP, :], spread_ref[c + k, edges - CAP:, :],
            ], axis=0) for k in range(2)
        ], axis=1)
        high = ends.astype(BF16)
        low = (ends - high.astype(F32)).astype(BF16)
        total = jnp.dot(
            end_summer, jnp.concatenate([high, low], axis=0), preferred_element_type=F32
        )
        for side in range(2):
            these = total[side * GSTR:(side + 1) * GSTR]
            given[side, c * GSTR:(c + 2) * GSTR, :] = jnp.concatenate(
                [these[:, :samples], these[:, samples:]], axis=0
            ).astype(BF16)

    has_lower = me > 0
    has_upper = me < n - 1

    def neighbour(side):
        return {"var": me - 1 if side == 0 else me + 1}

    def halo_copy(side, land):
        return pltpu.make_async_remote_copy(
            src_ref=given.at[side], dst_ref=taken.at[land],
            send_sem=halo_send.at[side], recv_sem=halo_recv.at[land],
            device_id=neighbour(side), device_id_type=MESH,
        )

    def own_copy(side, land):
        return pltpu.make_async_remote_copy(
            src_ref=lending.at[side], dst_ref=lent.at[land],
            send_sem=own_send.at[side], recv_sem=own_recv.at[land],
            device_id=neighbour(side), device_id_type=MESH,
        )

    inner = rows - 2 * edge

    def cdf_of(values):
        return 0.5 * (1.0 + lax.erf(values * root_half))

    def slopes_of(values, cdf):
        return cdf + values * jnp.exp(-0.5 * values * values) * inv_root_tau

    def own_work():
        for i in range(2, len(pieces)):
            wait_chunk(i)
            do_chunk(i)

        gene_at = lax.broadcasted_iota(jnp.int32, (rows, edges), 0)
        summer = (gene_at == id_row).astype(F32).astype(BF16)
        for c in range(0, CH, 2):
            both = jnp.concatenate(
                [spread_ref[c], spread_ref[c + 1]], axis=1
            )
            high = both.astype(BF16)
            low = (both - high.astype(F32)).astype(BF16)
            total = jnp.dot(summer, high, preferred_element_type=F32)
            total = total + jnp.dot(summer, low, preferred_element_type=F32)
            sums[c] = total[:, :samples]
            sums[c + 1] = total[:, samples:]
        share = jnp.zeros((8, samples), F32)
        for c in range(CH):
            values = sums[c, edge:rows - edge, :]
            cdf = cdf_of(values)
            cdfs[c, GSTR:genes - GSTR, :] = cdf
            hw = hw_wide[c, GSTR:genes - GSTR, :]
            share = share + jnp.sum((values * cdf * hw).reshape(inner // 8, 8, samples), axis=0)
        share_ref[...] = share

    def turn_dosage():
        for b in range(blocks):
            at = pl.ds(b * BLOCK, BLOCK)
            dose_ref[at, :] = dosage[:, at].T

    ahead = me < n // 8


    @pl.loop(0, 2)
    def _(step):
        @pl.when(step == 1 - ahead.astype(jnp.int32))
        def _():
            own_work()

            @pl.when(ahead)
            def _():
                turn_dosage()

        @pl.when(step == 0)
        def _():
            pl.semaphore_wait(barrier, n - 1)
            for side, there in ((0, has_lower), (1, has_upper)):
                @pl.when(there)
                def _(side=side):
                    halo_copy(side, 1 - side).start()

                @pl.when(jnp.logical_not(there))
                def _(side=side):
                    taken[side] = jnp.zeros(taken.shape[1:], BF16)
                    lent[side] = jnp.zeros(lent.shape[1:], BF16)

    share = share_ref[...]

    for side, there in ((0, has_lower), (1, has_upper)):
        @pl.when(there)
        def _(side=side):
            halo_copy(side, side).wait()

    for c in range(CH):
        for side in range(2):
            at = GSTR if side == 0 else rows - edge
            pair = taken[side, c // 2 * 2 * GSTR:(c // 2 + 1) * 2 * GSTR, :].astype(F32)
            values = sums[c, at:at + GSTR, :] + pair[c % 2 * GSTR:(c % 2 + 1) * GSTR]
            cdf = cdf_of(values)
            sums[c, at:at + GSTR, :] = values
            cdfs[c, at - GSTR:at, :] = cdf
            share = share + values * cdf * hw_wide[c, at - GSTR:at, :]

    mine[0] = jnp.sum(share, axis=0, keepdims=True)

    def share_copy(src, dst, other):
        return pltpu.make_async_remote_copy(
            src_ref=src, dst_ref=dst,
            send_sem=share_send, recv_sem=share_recv,
            device_id={"var": other}, device_id_type=MESH,
        )

    @pl.loop(0, n - 1)
    def _(j):
        other = j + (j >= me).astype(jnp.int32)
        share_copy(mine.at[0], shares.at[me], other).start()

    shares[me] = mine[0]

    for side in range(2):
        at = GSTR if side == 0 else rows - edge
        for c in range(0, CH, 2):
            pair = []
            for k in range(c, c + 2):
                values = sums[k, at:at + GSTR, :]
                hw = hw_wide[k, at - GSTR:at, :]
                pair.append(hw * slopes_of(values, cdfs[k, at - GSTR:at, :]))
            lending[side, c * GSTR:(c + 2) * GSTR, :] = jnp.concatenate(pair, axis=0).astype(BF16)

    for side, there in ((0, has_lower), (1, has_upper)):
        @pl.when(there)
        def _(side=side):
            own_copy(side, 1 - side).start()

    for c in range(CH):
        values = sums[c, GSTR:rows - GSTR, :]
        cdf = cdfs[c]
        hs_ref[c] = hw_wide[c] * slopes_of(values, cdf)
        act = values * cdf
        high = act.astype(BF16)
        act_ref[c, :samples, :] = high.T
        act_ref[c, samples:, :] = (act - high.astype(F32)).astype(BF16).T

    @pl.when(jnp.logical_not(ahead))
    def _():
        turn_dosage()

    tall = lax.dot_general(chosen, near, NT, preferred_element_type=F32)
    slot = lax.broadcasted_iota(jnp.int32, (edges, SLOTS), 1)
    sub = lax.broadcasted_iota(jnp.int32, (edges, SLOTS), 0)
    id_col = jnp.sum(jnp.where(sub % SLOTS == slot, tall, 0.0), axis=1, keepdims=True)
    id_col = id_col.astype(jnp.int32)
    gene_at = lax.broadcasted_iota(jnp.int32, (edges, genes), 1) + GSTR
    pick = (gene_at == id_col).astype(F32).astype(BF16)
    for c in range(0, CH, 2):
        both = jnp.concatenate([hs_ref[c], hs_ref[c + 1]], axis=1)
        high = both.astype(BF16)
        low = (both - high.astype(F32)).astype(BF16)
        picked = jnp.dot(pick, high, preferred_element_type=F32)
        picked = picked + jnp.dot(pick, low, preferred_element_type=F32)
        spread_ref[c] = picked[:, :samples]
        spread_ref[c + 1] = picked[:, samples:]

    def turn(b):
        these = jnp.swapaxes(spread_ref[:, pl.ds(b * SLOTS, SLOTS), :], 0, 1)
        turned_ref[b] = these.reshape(SLOTS * CH, samples).T

    for b in range(CAP // SLOTS, blocks - CAP // SLOTS):
        turn(b)

    column = lax.broadcasted_iota(jnp.int32, (2 * CAP, edge), 1)
    half = lax.broadcasted_iota(jnp.int32, (2 * CAP, edge), 0) // CAP
    for side, there in ((0, has_lower), (1, has_upper)):
        @pl.when(there)
        def _(side=side):
            own_copy(side, side).wait()

        skipped = side * (edges - CAP)
        id_ends = id_col[skipped:skipped + CAP]
        id_ends = jnp.concatenate([id_ends, id_ends], axis=0) - side * (rows - GSTR)
        end_pick = (id_ends == column - half * GSTR) & (column // GSTR == half)
        end_pick = end_pick.astype(F32).astype(BF16)
        for c in range(0, CH, 2):
            picked = jnp.dot(
                end_pick, lent[side, c * GSTR:(c + 2) * GSTR, :], preferred_element_type=F32
            )
            for k in range(2):
                at = pl.ds(skipped, CAP)
                spread_ref[c + k, at, :] = (
                    spread_ref[c + k, at, :] + picked[k * CAP:(k + 1) * CAP]
                )
        for b in range(CAP // SLOTS):
            turn(skipped // SLOTS + b)

    arrived = shares.at[pl.ds(0, n - 1)]
    share_copy(arrived, arrived, lax.rem(me + 1, n)).wait()

    logit_ref[...] = jnp.sum(shares[...], axis=0)


def backward_kernel(
    logit_ref, labels_ref, bias_ref, dose_ref, spread_ref, act_ref,
    grad_w_hbm, grad_head_hbm, totals_hbm, out, head, totals, out_sem, small_sem,
):
    samples = dose_ref.shape[1]
    blocks = out.shape[0]
    logits = logit_ref[...] + bias_ref[0]
    targets = labels_ref[...].astype(F32)
    dlogit = jax.nn.sigmoid(logits) - targets
    tall = jnp.broadcast_to(dlogit, (samples, samples)).T
    cuts = [blocks * p // OUT_PARTS[-1] for p in (0,) + OUT_PARTS]

    def out_copy(i):
        at = pl.ds(cuts[i], cuts[i + 1] - cuts[i])
        return pltpu.make_async_copy(out.at[at], grad_w_hbm.at[at], out_sem.at[i])

    for i in range(len(OUT_PARTS)):
        for b in range(cuts[i], cuts[i + 1]):
            grad_gene = (tall * spread_ref[b]).astype(BF16)
            out[b] = jnp.dot(
                dose_ref[pl.ds(b * BLOCK, BLOCK), :], grad_gene, preferred_element_type=F32
            )
        out_copy(i).start()

    loss = jnp.maximum(logits, 0.0) + jnp.log1p(jnp.exp(-jnp.abs(logits))) - targets * logits
    totals[0] = jnp.sum(loss)
    totals[1] = jnp.sum(dlogit)
    totals_copy = pltpu.make_async_copy(totals, totals_hbm, small_sem.at[0])
    totals_copy.start()

    top = dlogit.astype(BF16).astype(F32)
    middle = (dlogit - top).astype(BF16).astype(F32)
    rest = dlogit - top - middle
    row = lax.broadcasted_iota(jnp.int32, (8, samples), 0)
    parts = jnp.where(row == 0, top, jnp.where(row == 1, middle, jnp.where(row == 2, rest, 0.0)))
    parts = jnp.concatenate([parts, parts], axis=1).astype(BF16)
    for c in range(CH):
        found = jnp.dot(parts, act_ref[c], preferred_element_type=F32)
        head[c:c + 1, :] = jnp.sum(found, axis=0, keepdims=True)
    head_copy = pltpu.make_async_copy(head, grad_head_hbm, small_sem.at[1])
    head_copy.start()
    for i in range(len(OUT_PARTS)):
        out_copy(i).wait()
    totals_copy.wait()
    head_copy.wait()


def per_device(genotypes, labels, gene_weight, gene_idx, head_weight, head_bias):
    samples = genotypes.shape[0]
    blocks = gene_weight.shape[0]
    genes = head_weight.shape[0]
    rows = genes + 2 * GSTR
    n = lax.axis_size("var")
    vmem = pl.BlockSpec(memory_space=pltpu.VMEM)
    hbm = pl.BlockSpec(memory_space=pltpu.HBM)
    smem = pl.BlockSpec(memory_space=pltpu.SMEM)
    shape = jax.ShapeDtypeStruct
    dma = pltpu.SemaphoreType.DMA
    pieces = len(split_blocks(blocks))
    parts = len(OUT_PARTS)
    stay = functools.partial(pltpu.with_memory_space_constraint, memory_space=pltpu.HBM)
    dose, spread, act, logit = pl.pallas_call(
        functools.partial(forward_kernel, n),
        out_shape=(
            shape((blocks * BLOCK, samples), BF16),
            shape((blocks, samples, SLOTS * CH), F32),
            shape((CH, 2 * samples, genes), BF16),
            shape((1, samples), F32),
        ),
        in_specs=[hbm] * 4,
        out_specs=(vmem,) * 4,
        scratch_shapes=[
            pltpu.VMEM((CH, blocks * SLOTS, samples), F32),
            pltpu.VMEM((SLOTS, gene_idx.shape[0]), jnp.int32),
            pltpu.VMEM((CH, genes), F32),
            pltpu.VMEM((samples, blocks * BLOCK), jnp.int32),
            pltpu.VMEM((blocks, BLOCK, SLOTS * CH), BF16),
            pltpu.VMEM((samples, blocks * BLOCK), BF16),
            pltpu.VMEM((CH, genes, samples), F32),
            pltpu.VMEM((CH, genes, samples), F32),
            pltpu.VMEM((CH, rows, samples), F32),
            pltpu.VMEM((2, CH * GSTR, samples), BF16),
            pltpu.VMEM((2, CH * GSTR, samples), BF16),
            pltpu.VMEM((2, CH * GSTR, samples), BF16),
            pltpu.VMEM((2, CH * GSTR, samples), BF16),
            pltpu.VMEM((CH, genes, samples), F32),
            pltpu.VMEM((8, samples), F32),
            pltpu.VMEM((1, 1, samples), F32),
            pltpu.VMEM((n, 1, samples), F32),
            dma((pieces,)), dma((pieces,)), dma((2,)),
            dma((2,)), dma((2,)), dma((2,)), dma((2,)),
            dma, dma,
        ],
        compiler_params=pltpu.CompilerParams(
            collective_id=0, has_side_effects=True, vmem_limit_bytes=24 * 1024 * 1024
        ),
        name="forward",
    )(stay(gene_idx.T), stay(head_weight.T), stay(genotypes), stay(gene_weight))
    grad_w, grad_head, totals = pl.pallas_call(
        backward_kernel,
        out_shape=(
            shape((blocks, BLOCK, SLOTS * CH), F32),
            shape((CH, genes), F32),
            shape((2,), F32),
        ),
        in_specs=[vmem, vmem, smem, vmem, vmem, vmem],
        out_specs=(hbm, hbm, hbm),
        scratch_shapes=[
            pltpu.VMEM((blocks, BLOCK, SLOTS * CH), F32),
            pltpu.VMEM((CH, genes), F32),
            pltpu.SMEM((2,), F32),
            dma((parts,)), dma((2,)),
        ],
        compiler_params=pltpu.CompilerParams(vmem_limit_bytes=24 * 1024 * 1024),
        name="backward",
    )(logit, labels.reshape(1, samples), head_bias, dose, spread, act)
    return (grad_w, grad_head.T, totals)


def solution(mesh):
    placed = (P("grp", "var"), P("grp"), P("var", None, None), P(), P("var", None), P())
    return jax.shard_map(
        per_device,
        mesh=mesh,
        in_specs=placed,
        out_specs=(P(("grp", "var"), None, None), P(("grp", "var"), None), P("grp")),
        check_vma=False,
    )
```

```python
import functools

import jax
import jax.numpy as jnp
from jax import lax
from jax.experimental import pallas as pl
from jax.experimental.pallas import tpu as pltpu
from jax.sharding import PartitionSpec as P

CH = 16
BLOCK = 128
SLOTS = 8
GSTR = 8
CAP = 32
OUT_PARTS = (2, 6, 12, 18, 24, 30)

root_half = 0.7071067811865476
inv_root_tau = 0.3989422804014327

MESH = pl.DeviceIdType.MESH
F32 = jnp.float32
BF16 = jnp.bfloat16
NT = (((1,), (1,)), ((), ()))


def split_blocks(blocks):
    end = CAP // SLOTS
    inner = blocks - 2 * end
    cuts = [end, end + inner]
    return [(0, end), (blocks - end, end)] + [(p, q - p) for p, q in zip(cuts, cuts[1:])]


def forward_kernel(
    n, ids_hbm, hw_hbm, geno_hbm, w_hbm,
    dose_ref, turned_ref, act_ref, logit_ref,
    spread_ref, ids_ref, hw_ref, geno, weight, dosage, hs_ref, cdfs, sums, given, taken, lending, lent, hw_wide, share_ref, mine, shares,
    geno_sem, w_sem, small_sem, halo_send, halo_recv, own_send, own_recv, share_send, share_recv,
):
    me = lax.axis_index("var")
    samples = geno.shape[0]
    blocks = weight.shape[0]
    genes = hw_ref.shape[1]
    rows = genes + 2 * GSTR
    edges = blocks * SLOTS
    all_blocks = ids_ref.shape[1]
    edge = 2 * GSTR

    barrier = pltpu.get_barrier_semaphore()

    pieces = split_blocks(blocks)

    def geno_copy(i):
        first, count = pieces[i]
        cols = pl.ds(first * BLOCK, count * BLOCK)
        return pltpu.make_async_copy(geno_hbm.at[:, cols], geno.at[:, cols], geno_sem.at[i])

    def w_copy(i):
        at = pl.ds(*pieces[i])
        return pltpu.make_async_copy(w_hbm.at[at], weight.at[at], w_sem.at[i])

    ids_copy = pltpu.make_async_copy(ids_hbm, ids_ref, small_sem.at[0])
    hw_load = pltpu.make_async_copy(hw_hbm, hw_ref, small_sem.at[1])
    ids_copy.start()
    hw_load.start()
    for i in range(len(pieces)):
        geno_copy(i).start()
        w_copy(i).start()
        if i == 0:
            def greet(j):
                pl.semaphore_signal(
                    barrier, inc=1, device_id={"var": lax.rem(me + j, n)}, device_id_type=MESH
                )

            greet(n - 1)
            greet(1)

            @pl.loop(2, n - 1)
            def _(j):
                greet(j)


    def wait_chunk(i):
        geno_copy(i).wait()
        w_copy(i).wait()

    def do_chunk(i):
        for b in range(pieces[i][0], sum(pieces[i])):
            at = pl.ds(b * BLOCK, BLOCK)
            dose = geno[:, at].astype(F32).astype(BF16)
            dosage[:, at] = dose
            found = lax.dot_general(
                weight[b], dose, (((0,), (1,)), ((), ())), preferred_element_type=F32
            )
            found = jnp.swapaxes(found.reshape(SLOTS, CH, samples), 0, 1)
            spread_ref[:, pl.ds(b * SLOTS, SLOTS), :] = found

    hw_load.wait()
    hw_own = hw_ref[...].T
    for c in range(CH):
        hw_wide[c] = jnp.broadcast_to(hw_own[:, c:c + 1], (genes, samples))
    ids_copy.wait()
    wait_chunk(0)
    wait_chunk(1)
    first = me * genes - GSTR
    ids = ids_ref[...]
    width = -(-all_blocks // 128) * 128
    if width > all_blocks:
        ids = jnp.concatenate([ids, jnp.zeros((SLOTS, width - all_blocks), jnp.int32)], axis=1)
    near = pltpu.roll(ids, lax.rem(width - me * blocks, width), 1)[:, :128] - first
    near = near.astype(F32).astype(BF16)
    chosen = (
        lax.broadcasted_iota(jnp.int32, (edges, 128), 1)
        == lax.broadcasted_iota(jnp.int32, (edges, 128), 0) // SLOTS
    ).astype(F32).astype(BF16)
    wide = lax.dot_general(near, chosen, NT, preferred_element_type=F32)
    slot = lax.broadcasted_iota(jnp.int32, (SLOTS, edges), 0)
    lane = lax.broadcasted_iota(jnp.int32, (SLOTS, edges), 1)
    id_row = jnp.sum(jnp.where(lane % SLOTS == slot, wide, 0.0), axis=0, keepdims=True)
    id_row = id_row.astype(jnp.int32)

    id_ends = jnp.concatenate([id_row[:, :CAP], id_row[:, edges - CAP:]], axis=1)
    id_ends = jnp.concatenate([id_ends, id_ends], axis=1)
    end_at = lax.broadcasted_iota(jnp.int32, (edge, 4 * CAP), 0)
    end_at = jnp.where(end_at < GSTR, end_at, end_at + (rows - edge))
    end_summer = (end_at == id_ends).astype(F32).astype(BF16)

    do_chunk(0)
    do_chunk(1)

    for c in range(0, CH, 2):
        ends = jnp.concatenate([
            jnp.concatenate([
                spread_ref[c + k, :CAP, :], spread_ref[c + k, edges - CAP:, :],
            ], axis=0) for k in range(2)
        ], axis=1)
        high = ends.astype(BF16)
        low = (ends - high.astype(F32)).astype(BF16)
        total = jnp.dot(
            end_summer, jnp.concatenate([high, low], axis=0), preferred_element_type=F32
        )
        for side in range(2):
            these = total[side * GSTR:(side + 1) * GSTR]
            given[side, c * GSTR:(c + 2) * GSTR, :] = jnp.concatenate(
                [these[:, :samples], these[:, samples:]], axis=0
            ).astype(BF16)

    has_lower = me > 0
    has_upper = me < n - 1

    def neighbour(side):
        return {"var": me - 1 if side == 0 else me + 1}

    def halo_copy(side, land):
        return pltpu.make_async_remote_copy(
            src_ref=given.at[side], dst_ref=taken.at[land],
            send_sem=halo_send.at[side], recv_sem=halo_recv.at[land],
            device_id=neighbour(side), device_id_type=MESH,
        )

    def own_copy(side, land):
        return pltpu.make_async_remote_copy(
            src_ref=lending.at[side], dst_ref=lent.at[land],
            send_sem=own_send.at[side], recv_sem=own_recv.at[land],
            device_id=neighbour(side), device_id_type=MESH,
        )

    inner = rows - 2 * edge

    def cdf_of(values):
        return 0.5 * (1.0 + lax.erf(values * root_half))

    def slopes_of(values, cdf):
        return cdf + values * jnp.exp(-0.5 * values * values) * inv_root_tau

    def own_work():
        for i in range(2, len(pieces)):
            wait_chunk(i)
            do_chunk(i)

        gene_at = lax.broadcasted_iota(jnp.int32, (rows, edges), 0)
        summer = (gene_at == id_row).astype(F32).astype(BF16)
        for c in range(0, CH, 2):
            both = jnp.concatenate(
                [spread_ref[c], spread_ref[c + 1]], axis=1
            )
            high = both.astype(BF16)
            low = (both - high.astype(F32)).astype(BF16)
            total = jnp.dot(summer, high, preferred_element_type=F32)
            total = total + jnp.dot(summer, low, preferred_element_type=F32)
            sums[c] = total[:, :samples]
            sums[c + 1] = total[:, samples:]
        share = jnp.zeros((8, samples), F32)
        for c in range(CH):
            values = sums[c, edge:rows - edge, :]
            cdf = cdf_of(values)
            cdfs[c, GSTR:genes - GSTR, :] = cdf
            hw = hw_wide[c, GSTR:genes - GSTR, :]
            share = share + jnp.sum((values * cdf * hw).reshape(inner // 8, 8, samples), axis=0)
        share_ref[...] = share

    def turn_dosage():
        for b in range(blocks):
            at = pl.ds(b * BLOCK, BLOCK)
            dose_ref[at, :] = dosage[:, at].T

    ahead = me < n // 8


    @pl.loop(0, 2)
    def _(step):
        @pl.when(step == 1 - ahead.astype(jnp.int32))
        def _():
            own_work()

            @pl.when(ahead)
            def _():
                turn_dosage()

        @pl.when(step == 0)
        def _():
            pl.semaphore_wait(barrier, n - 1)
            for side, there in ((0, has_lower), (1, has_upper)):
                @pl.when(there)
                def _(side=side):
                    halo_copy(side, 1 - side).start()

                @pl.when(jnp.logical_not(there))
                def _(side=side):
                    taken[side] = jnp.zeros(taken.shape[1:], BF16)
                    lent[side] = jnp.zeros(lent.shape[1:], BF16)

    share = share_ref[...]

    for side, there in ((0, has_lower), (1, has_upper)):
        @pl.when(there)
        def _(side=side):
            halo_copy(side, side).wait()

    for c in range(CH):
        for side in range(2):
            at = GSTR if side == 0 else rows - edge
            pair = taken[side, c // 2 * 2 * GSTR:(c // 2 + 1) * 2 * GSTR, :].astype(F32)
            values = sums[c, at:at + GSTR, :] + pair[c % 2 * GSTR:(c % 2 + 1) * GSTR]
            cdf = cdf_of(values)
            sums[c, at:at + GSTR, :] = values
            cdfs[c, at - GSTR:at, :] = cdf
            share = share + values * cdf * hw_wide[c, at - GSTR:at, :]

    mine[0] = jnp.sum(share, axis=0, keepdims=True)

    def share_copy(src, dst, other):
        return pltpu.make_async_remote_copy(
            src_ref=src, dst_ref=dst,
            send_sem=share_send, recv_sem=share_recv,
            device_id={"var": other}, device_id_type=MESH,
        )

    @pl.loop(0, n - 1, unroll=3 if n % 3 == 1 else 1)
    def _(j):
        other = j + (j >= me).astype(jnp.int32)
        share_copy(mine.at[0], shares.at[me], other).start()

    shares[me] = mine[0]

    for side in range(2):
        at = GSTR if side == 0 else rows - edge
        for c in range(0, CH, 2):
            pair = []
            for k in range(c, c + 2):
                values = sums[k, at:at + GSTR, :]
                hw = hw_wide[k, at - GSTR:at, :]
                pair.append(hw * slopes_of(values, cdfs[k, at - GSTR:at, :]))
            lending[side, c * GSTR:(c + 2) * GSTR, :] = jnp.concatenate(pair, axis=0).astype(BF16)

    for side, there in ((0, has_lower), (1, has_upper)):
        @pl.when(there)
        def _(side=side):
            own_copy(side, 1 - side).start()

    for c in range(CH):
        values = sums[c, GSTR:rows - GSTR, :]
        cdf = cdfs[c]
        hs_ref[c] = hw_wide[c] * slopes_of(values, cdf)
        act = values * cdf
        high = act.astype(BF16)
        act_ref[c, :samples, :] = high.T
        act_ref[c, samples:, :] = (act - high.astype(F32)).astype(BF16).T

    @pl.when(jnp.logical_not(ahead))
    def _():
        turn_dosage()

    tall = lax.dot_general(chosen, near, NT, preferred_element_type=F32)
    slot = lax.broadcasted_iota(jnp.int32, (edges, SLOTS), 1)
    sub = lax.broadcasted_iota(jnp.int32, (edges, SLOTS), 0)
    id_col = jnp.sum(jnp.where(sub % SLOTS == slot, tall, 0.0), axis=1, keepdims=True)
    id_col = id_col.astype(jnp.int32)
    gene_at = lax.broadcasted_iota(jnp.int32, (edges, genes), 1) + GSTR
    pick = (gene_at == id_col).astype(F32).astype(BF16)
    for c in range(0, CH, 2):
        both = jnp.concatenate([hs_ref[c], hs_ref[c + 1]], axis=1)
        high = both.astype(BF16)
        low = (both - high.astype(F32)).astype(BF16)
        picked = jnp.dot(pick, high, preferred_element_type=F32)
        picked = picked + jnp.dot(pick, low, preferred_element_type=F32)
        spread_ref[c] = picked[:, :samples]
        spread_ref[c + 1] = picked[:, samples:]

    def turn(b):
        these = jnp.swapaxes(spread_ref[:, pl.ds(b * SLOTS, SLOTS), :], 0, 1)
        turned_ref[b] = these.reshape(SLOTS * CH, samples).T

    for b in range(CAP // SLOTS, blocks - CAP // SLOTS):
        turn(b)

    column = lax.broadcasted_iota(jnp.int32, (2 * CAP, edge), 1)
    half = lax.broadcasted_iota(jnp.int32, (2 * CAP, edge), 0) // CAP
    for side, there in ((0, has_lower), (1, has_upper)):
        @pl.when(there)
        def _(side=side):
            own_copy(side, side).wait()

        skipped = side * (edges - CAP)
        id_ends = id_col[skipped:skipped + CAP]
        id_ends = jnp.concatenate([id_ends, id_ends], axis=0) - side * (rows - GSTR)
        end_pick = (id_ends == column - half * GSTR) & (column // GSTR == half)
        end_pick = end_pick.astype(F32).astype(BF16)
        for c in range(0, CH, 2):
            picked = jnp.dot(
                end_pick, lent[side, c * GSTR:(c + 2) * GSTR, :], preferred_element_type=F32
            )
            for k in range(2):
                at = pl.ds(skipped, CAP)
                spread_ref[c + k, at, :] = (
                    spread_ref[c + k, at, :] + picked[k * CAP:(k + 1) * CAP]
                )
        for b in range(CAP // SLOTS):
            turn(skipped // SLOTS + b)

    arrived = shares.at[pl.ds(0, n - 1)]
    share_copy(arrived, arrived, lax.rem(me + 1, n)).wait()

    logit_ref[...] = jnp.sum(shares[...], axis=0)


def backward_kernel(
    logit_ref, labels_ref, bias_ref, dose_ref, spread_ref, act_ref,
    grad_w_hbm, grad_head_hbm, totals_hbm, out, head, totals, out_sem, small_sem,
):
    samples = dose_ref.shape[1]
    blocks = out.shape[0]
    logits = logit_ref[...] + bias_ref[0]
    targets = labels_ref[...].astype(F32)
    dlogit = jax.nn.sigmoid(logits) - targets
    tall = jnp.broadcast_to(dlogit, (samples, samples)).T
    cuts = [blocks * p // OUT_PARTS[-1] for p in (0,) + OUT_PARTS]

    def out_copy(i):
        at = pl.ds(cuts[i], cuts[i + 1] - cuts[i])
        return pltpu.make_async_copy(out.at[at], grad_w_hbm.at[at], out_sem.at[i])

    for i in range(len(OUT_PARTS)):
        for b in range(cuts[i], cuts[i + 1]):
            grad_gene = (tall * spread_ref[b]).astype(BF16)
            out[b] = jnp.dot(
                dose_ref[pl.ds(b * BLOCK, BLOCK), :], grad_gene, preferred_element_type=F32
            )
        out_copy(i).start()

    loss = jnp.maximum(logits, 0.0) + jnp.log1p(jnp.exp(-jnp.abs(logits))) - targets * logits
    totals[0] = jnp.sum(loss)
    totals[1] = jnp.sum(dlogit)
    totals_copy = pltpu.make_async_copy(totals, totals_hbm, small_sem.at[0])
    totals_copy.start()

    top = dlogit.astype(BF16).astype(F32)
    middle = (dlogit - top).astype(BF16).astype(F32)
    rest = dlogit - top - middle
    row = lax.broadcasted_iota(jnp.int32, (8, samples), 0)
    parts = jnp.where(row == 0, top, jnp.where(row == 1, middle, jnp.where(row == 2, rest, 0.0)))
    parts = jnp.concatenate([parts, parts], axis=1).astype(BF16)
    for c in range(CH):
        found = jnp.dot(parts, act_ref[c], preferred_element_type=F32)
        head[c:c + 1, :] = jnp.sum(found, axis=0, keepdims=True)
    head_copy = pltpu.make_async_copy(head, grad_head_hbm, small_sem.at[1])
    head_copy.start()
    for i in range(len(OUT_PARTS)):
        out_copy(i).wait()
    totals_copy.wait()
    head_copy.wait()


def per_device(genotypes, labels, gene_weight, gene_idx, head_weight, head_bias):
    samples = genotypes.shape[0]
    blocks = gene_weight.shape[0]
    genes = head_weight.shape[0]
    rows = genes + 2 * GSTR
    n = lax.axis_size("var")
    vmem = pl.BlockSpec(memory_space=pltpu.VMEM)
    hbm = pl.BlockSpec(memory_space=pltpu.HBM)
    smem = pl.BlockSpec(memory_space=pltpu.SMEM)
    shape = jax.ShapeDtypeStruct
    dma = pltpu.SemaphoreType.DMA
    pieces = len(split_blocks(blocks))
    parts = len(OUT_PARTS)
    stay = functools.partial(pltpu.with_memory_space_constraint, memory_space=pltpu.HBM)
    dose, spread, act, logit = pl.pallas_call(
        functools.partial(forward_kernel, n),
        out_shape=(
            shape((blocks * BLOCK, samples), BF16),
            shape((blocks, samples, SLOTS * CH), F32),
            shape((CH, 2 * samples, genes), BF16),
            shape((1, samples), F32),
        ),
        in_specs=[hbm] * 4,
        out_specs=(vmem,) * 4,
        scratch_shapes=[
            pltpu.VMEM((CH, blocks * SLOTS, samples), F32),
            pltpu.VMEM((SLOTS, gene_idx.shape[0]), jnp.int32),
            pltpu.VMEM((CH, genes), F32),
            pltpu.VMEM((samples, blocks * BLOCK), jnp.int32),
            pltpu.VMEM((blocks, BLOCK, SLOTS * CH), BF16),
            pltpu.VMEM((samples, blocks * BLOCK), BF16),
            pltpu.VMEM((CH, genes, samples), F32),
            pltpu.VMEM((CH, genes, samples), F32),
            pltpu.VMEM((CH, rows, samples), F32),
            pltpu.VMEM((2, CH * GSTR, samples), BF16),
            pltpu.VMEM((2, CH * GSTR, samples), BF16),
            pltpu.VMEM((2, CH * GSTR, samples), BF16),
            pltpu.VMEM((2, CH * GSTR, samples), BF16),
            pltpu.VMEM((CH, genes, samples), F32),
            pltpu.VMEM((8, samples), F32),
            pltpu.VMEM((1, 1, samples), F32),
            pltpu.VMEM((n, 1, samples), F32),
            dma((pieces,)), dma((pieces,)), dma((2,)),
            dma((2,)), dma((2,)), dma((2,)), dma((2,)),
            dma, dma,
        ],
        compiler_params=pltpu.CompilerParams(
            collective_id=0, has_side_effects=True, vmem_limit_bytes=24 * 1024 * 1024
        ),
        name="forward",
    )(stay(gene_idx.T), stay(head_weight.T), stay(genotypes), stay(gene_weight))
    grad_w, grad_head, totals = pl.pallas_call(
        backward_kernel,
        out_shape=(
            shape((blocks, BLOCK, SLOTS * CH), F32),
            shape((CH, genes), F32),
            shape((2,), F32),
        ),
        in_specs=[vmem, vmem, smem, vmem, vmem, vmem],
        out_specs=(hbm, hbm, hbm),
        scratch_shapes=[
            pltpu.VMEM((blocks, BLOCK, SLOTS * CH), F32),
            pltpu.VMEM((CH, genes), F32),
            pltpu.SMEM((2,), F32),
            dma((parts,)), dma((2,)),
        ],
        compiler_params=pltpu.CompilerParams(vmem_limit_bytes=24 * 1024 * 1024),
        name="backward",
    )(logit, labels.reshape(1, samples), head_bias, dose, spread, act)
    return (grad_w, grad_head.T, totals)


def solution(mesh):
    placed = (P("grp", "var"), P("grp"), P("var", None, None), P(), P("var", None), P())
    return jax.shard_map(
        per_device,
        mesh=mesh,
        in_specs=placed,
        out_specs=(P(("grp", "var"), None, None), P(("grp", "var"), None), P("grp")),
        check_vma=False,
    )
```

```python
import functools

import jax
import jax.numpy as jnp
from jax import lax
from jax.experimental import pallas as pl
from jax.experimental.pallas import tpu as pltpu
from jax.sharding import PartitionSpec as P

CH = 16
BLOCK = 128
SLOTS = 8
GSTR = 8
CAP = 32
OUT_PARTS = (2, 6, 12, 18, 24, 30)

root_half = 0.7071067811865476
inv_root_tau = 0.3989422804014327

MESH = pl.DeviceIdType.MESH
F32 = jnp.float32
BF16 = jnp.bfloat16
NT = (((1,), (1,)), ((), ()))


def split_blocks(blocks):
    end = CAP // SLOTS
    inner = blocks - 2 * end
    cuts = [end + inner * k // 2 for k in range(3)]
    return [(0, end), (blocks - end, end)] + [(p, q - p) for p, q in zip(cuts, cuts[1:])]


def forward_kernel(
    n, ids_hbm, hw_hbm, geno_hbm, w_hbm,
    dose_ref, turned_ref, act_ref, logit_ref,
    spread_ref, ids_ref, hw_ref, geno, weight, dosage, hs_ref, cdfs, sums, given, taken, lending, lent, hw_wide, share_ref, mine, shares,
    geno_sem, w_sem, small_sem, halo_send, halo_recv, own_send, own_recv, share_send, share_recv,
):
    me = lax.axis_index("var")
    samples = geno.shape[0]
    blocks = weight.shape[0]
    genes = hw_ref.shape[1]
    rows = genes + 2 * GSTR
    edges = blocks * SLOTS
    all_blocks = ids_ref.shape[1]
    edge = 2 * GSTR

    barrier = pltpu.get_barrier_semaphore()

    pieces = split_blocks(blocks)

    def geno_copy(i):
        first, count = pieces[i]
        cols = pl.ds(first * BLOCK, count * BLOCK)
        return pltpu.make_async_copy(geno_hbm.at[:, cols], geno.at[:, cols], geno_sem.at[i])

    def w_copy(i):
        at = pl.ds(*pieces[i])
        return pltpu.make_async_copy(w_hbm.at[at], weight.at[at], w_sem.at[i])

    ids_copy = pltpu.make_async_copy(ids_hbm, ids_ref, small_sem.at[0])
    hw_load = pltpu.make_async_copy(hw_hbm, hw_ref, small_sem.at[1])
    ids_copy.start()
    hw_load.start()
    for i in range(len(pieces)):
        geno_copy(i).start()
        w_copy(i).start()
        if i == 0:
            def greet(j):
                pl.semaphore_signal(
                    barrier, inc=1, device_id={"var": lax.rem(me + j, n)}, device_id_type=MESH
                )

            greet(n - 1)
            greet(1)

            @pl.loop(2, n - 1)
            def _(j):
                greet(j)


    def wait_chunk(i):
        geno_copy(i).wait()
        w_copy(i).wait()

    def do_chunk(i):
        for b in range(pieces[i][0], sum(pieces[i])):
            at = pl.ds(b * BLOCK, BLOCK)
            dose = geno[:, at].astype(F32).astype(BF16)
            dosage[:, at] = dose
            found = lax.dot_general(
                weight[b], dose, (((0,), (1,)), ((), ())), preferred_element_type=F32
            )
            found = jnp.swapaxes(found.reshape(SLOTS, CH, samples), 0, 1)
            spread_ref[:, pl.ds(b * SLOTS, SLOTS), :] = found

    hw_load.wait()
    hw_own = hw_ref[...].T
    for c in range(CH):
        hw_wide[c] = jnp.broadcast_to(hw_own[:, c:c + 1], (genes, samples))
    ids_copy.wait()
    wait_chunk(0)
    wait_chunk(1)
    first = me * genes - GSTR
    ids = ids_ref[...]
    width = -(-all_blocks // 128) * 128
    if width > all_blocks:
        ids = jnp.concatenate([ids, jnp.zeros((SLOTS, width - all_blocks), jnp.int32)], axis=1)
    near = pltpu.roll(ids, lax.rem(width - me * blocks, width), 1)[:, :128] - first
    near = near.astype(F32).astype(BF16)
    chosen = (
        lax.broadcasted_iota(jnp.int32, (edges, 128), 1)
        == lax.broadcasted_iota(jnp.int32, (edges, 128), 0) // SLOTS
    ).astype(F32).astype(BF16)
    wide = lax.dot_general(near, chosen, NT, preferred_element_type=F32)
    slot = lax.broadcasted_iota(jnp.int32, (SLOTS, edges), 0)
    lane = lax.broadcasted_iota(jnp.int32, (SLOTS, edges), 1)
    id_row = jnp.sum(jnp.where(lane % SLOTS == slot, wide, 0.0), axis=0, keepdims=True)
    id_row = id_row.astype(jnp.int32)

    id_ends = jnp.concatenate([id_row[:, :CAP], id_row[:, edges - CAP:]], axis=1)
    id_ends = jnp.concatenate([id_ends, id_ends], axis=1)
    end_at = lax.broadcasted_iota(jnp.int32, (edge, 4 * CAP), 0)
    end_at = jnp.where(end_at < GSTR, end_at, end_at + (rows - edge))
    end_summer = (end_at == id_ends).astype(F32).astype(BF16)

    do_chunk(0)
    do_chunk(1)

    for c in range(0, CH, 2):
        ends = jnp.concatenate([
            jnp.concatenate([
                spread_ref[c + k, :CAP, :], spread_ref[c + k, edges - CAP:, :],
            ], axis=0) for k in range(2)
        ], axis=1)
        high = ends.astype(BF16)
        low = (ends - high.astype(F32)).astype(BF16)
        total = jnp.dot(
            end_summer, jnp.concatenate([high, low], axis=0), preferred_element_type=F32
        )
        for side in range(2):
            these = total[side * GSTR:(side + 1) * GSTR]
            given[side, c * GSTR:(c + 2) * GSTR, :] = jnp.concatenate(
                [these[:, :samples], these[:, samples:]], axis=0
            ).astype(BF16)

    has_lower = me > 0
    has_upper = me < n - 1

    def neighbour(side):
        return {"var": me - 1 if side == 0 else me + 1}

    def halo_copy(side, land):
        return pltpu.make_async_remote_copy(
            src_ref=given.at[side], dst_ref=taken.at[land],
            send_sem=halo_send.at[side], recv_sem=halo_recv.at[land],
            device_id=neighbour(side), device_id_type=MESH,
        )

    def own_copy(side, land):
        return pltpu.make_async_remote_copy(
            src_ref=lending.at[side], dst_ref=lent.at[land],
            send_sem=own_send.at[side], recv_sem=own_recv.at[land],
            device_id=neighbour(side), device_id_type=MESH,
        )

    inner = rows - 2 * edge

    def cdf_of(values):
        return 0.5 * (1.0 + lax.erf(values * root_half))

    def slopes_of(values, cdf):
        return cdf + values * jnp.exp(-0.5 * values * values) * inv_root_tau

    def own_work():
        for i in range(2, len(pieces)):
            wait_chunk(i)
            do_chunk(i)

        gene_at = lax.broadcasted_iota(jnp.int32, (rows, edges), 0)
        summer = (gene_at == id_row).astype(F32).astype(BF16)
        for c in range(0, CH, 2):
            both = jnp.concatenate(
                [spread_ref[c], spread_ref[c + 1]], axis=1
            )
            high = both.astype(BF16)
            low = (both - high.astype(F32)).astype(BF16)
            total = jnp.dot(summer, high, preferred_element_type=F32)
            total = total + jnp.dot(summer, low, preferred_element_type=F32)
            sums[c] = total[:, :samples]
            sums[c + 1] = total[:, samples:]
        share = jnp.zeros((8, samples), F32)
        for c in range(CH):
            values = sums[c, edge:rows - edge, :]
            cdf = cdf_of(values)
            cdfs[c, GSTR:genes - GSTR, :] = cdf
            hw = hw_wide[c, GSTR:genes - GSTR, :]
            share = share + jnp.sum((values * cdf * hw).reshape(inner // 8, 8, samples), axis=0)
        share_ref[...] = share

    def turn_dosage():
        for b in range(blocks):
            at = pl.ds(b * BLOCK, BLOCK)
            dose_ref[at, :] = dosage[:, at].T

    ahead = me < n // 8


    @pl.loop(0, 2)
    def _(step):
        @pl.when(step == 1 - ahead.astype(jnp.int32))
        def _():
            own_work()

            @pl.when(ahead)
            def _():
                turn_dosage()

        @pl.when(step == 0)
        def _():
            pl.semaphore_wait(barrier, n - 1)
            for side, there in ((0, has_lower), (1, has_upper)):
                @pl.when(there)
                def _(side=side):
                    halo_copy(side, 1 - side).start()

                @pl.when(jnp.logical_not(there))
                def _(side=side):
                    taken[side] = jnp.zeros(taken.shape[1:], BF16)
                    lent[side] = jnp.zeros(lent.shape[1:], BF16)

    share = share_ref[...]

    for side, there in ((0, has_lower), (1, has_upper)):
        @pl.when(there)
        def _(side=side):
            halo_copy(side, side).wait()

    for c in range(CH):
        for side in range(2):
            at = GSTR if side == 0 else rows - edge
            pair = taken[side, c // 2 * 2 * GSTR:(c // 2 + 1) * 2 * GSTR, :].astype(F32)
            values = sums[c, at:at + GSTR, :] + pair[c % 2 * GSTR:(c % 2 + 1) * GSTR]
            cdf = cdf_of(values)
            sums[c, at:at + GSTR, :] = values
            cdfs[c, at - GSTR:at, :] = cdf
            share = share + values * cdf * hw_wide[c, at - GSTR:at, :]

    mine[0] = jnp.sum(share, axis=0, keepdims=True)

    def share_copy(src, dst, other):
        return pltpu.make_async_remote_copy(
            src_ref=src, dst_ref=dst,
            send_sem=share_send, recv_sem=share_recv,
            device_id={"var": other}, device_id_type=MESH,
        )

    @pl.loop(0, n - 1, unroll=3 if n % 3 == 1 else 1)
    def _(j):
        other = j + (j >= me).astype(jnp.int32)
        share_copy(mine.at[0], shares.at[me], other).start()

    shares[me] = mine[0]

    for side in range(2):
        at = GSTR if side == 0 else rows - edge
        for c in range(0, CH, 2):
            pair = []
            for k in range(c, c + 2):
                values = sums[k, at:at + GSTR, :]
                hw = hw_wide[k, at - GSTR:at, :]
                pair.append(hw * slopes_of(values, cdfs[k, at - GSTR:at, :]))
            lending[side, c * GSTR:(c + 2) * GSTR, :] = jnp.concatenate(pair, axis=0).astype(BF16)

    for side, there in ((0, has_lower), (1, has_upper)):
        @pl.when(there)
        def _(side=side):
            own_copy(side, 1 - side).start()

    for c in range(CH):
        values = sums[c, GSTR:rows - GSTR, :]
        cdf = cdfs[c]
        hs_ref[c] = hw_wide[c] * slopes_of(values, cdf)
        act = values * cdf
        high = act.astype(BF16)
        act_ref[c, :samples, :] = high.T
        act_ref[c, samples:, :] = (act - high.astype(F32)).astype(BF16).T

    @pl.when(jnp.logical_not(ahead))
    def _():
        turn_dosage()

    tall = lax.dot_general(chosen, near, NT, preferred_element_type=F32)
    slot = lax.broadcasted_iota(jnp.int32, (edges, SLOTS), 1)
    sub = lax.broadcasted_iota(jnp.int32, (edges, SLOTS), 0)
    id_col = jnp.sum(jnp.where(sub % SLOTS == slot, tall, 0.0), axis=1, keepdims=True)
    id_col = id_col.astype(jnp.int32)
    gene_at = lax.broadcasted_iota(jnp.int32, (edges, genes), 1) + GSTR
    pick = (gene_at == id_col).astype(F32).astype(BF16)
    for c in range(0, CH, 2):
        both = jnp.concatenate([hs_ref[c], hs_ref[c + 1]], axis=1)
        high = both.astype(BF16)
        low = (both - high.astype(F32)).astype(BF16)
        picked = jnp.dot(pick, high, preferred_element_type=F32)
        picked = picked + jnp.dot(pick, low, preferred_element_type=F32)
        spread_ref[c] = picked[:, :samples]
        spread_ref[c + 1] = picked[:, samples:]

    def turn(b):
        these = jnp.swapaxes(spread_ref[:, pl.ds(b * SLOTS, SLOTS), :], 0, 1)
        turned_ref[b] = these.reshape(SLOTS * CH, samples).T

    for b in range(CAP // SLOTS, blocks - CAP // SLOTS):
        turn(b)

    column = lax.broadcasted_iota(jnp.int32, (2 * CAP, edge), 1)
    half = lax.broadcasted_iota(jnp.int32, (2 * CAP, edge), 0) // CAP
    for side, there in ((0, has_lower), (1, has_upper)):
        @pl.when(there)
        def _(side=side):
            own_copy(side, side).wait()

        skipped = side * (edges - CAP)
        id_ends = id_col[skipped:skipped + CAP]
        id_ends = jnp.concatenate([id_ends, id_ends], axis=0) - side * (rows - GSTR)
        end_pick = (id_ends == column - half * GSTR) & (column // GSTR == half)
        end_pick = end_pick.astype(F32).astype(BF16)
        for c in range(0, CH, 2):
            picked = jnp.dot(
                end_pick, lent[side, c * GSTR:(c + 2) * GSTR, :], preferred_element_type=F32
            )
            for k in range(2):
                at = pl.ds(skipped, CAP)
                spread_ref[c + k, at, :] = (
                    spread_ref[c + k, at, :] + picked[k * CAP:(k + 1) * CAP]
                )
        for b in range(CAP // SLOTS):
            turn(skipped // SLOTS + b)

    arrived = shares.at[pl.ds(0, n - 1)]
    share_copy(arrived, arrived, lax.rem(me + 1, n)).wait()

    logit_ref[...] = jnp.sum(shares[...], axis=0)


def backward_kernel(
    logit_ref, labels_ref, bias_ref, dose_ref, spread_ref, act_ref,
    grad_w_hbm, grad_head_hbm, totals_hbm, out, head, totals, out_sem, small_sem,
):
    samples = dose_ref.shape[1]
    blocks = out.shape[0]
    logits = logit_ref[...] + bias_ref[0]
    targets = labels_ref[...].astype(F32)
    dlogit = jax.nn.sigmoid(logits) - targets
    tall = jnp.broadcast_to(dlogit, (samples, samples)).T
    cuts = [blocks * p // OUT_PARTS[-1] for p in (0,) + OUT_PARTS]

    def out_copy(i):
        at = pl.ds(cuts[i], cuts[i + 1] - cuts[i])
        return pltpu.make_async_copy(out.at[at], grad_w_hbm.at[at], out_sem.at[i])

    for i in range(len(OUT_PARTS)):
        for b in range(cuts[i], cuts[i + 1]):
            grad_gene = (tall * spread_ref[b]).astype(BF16)
            out[b] = jnp.dot(
                dose_ref[pl.ds(b * BLOCK, BLOCK), :], grad_gene, preferred_element_type=F32
            )
        out_copy(i).start()

    loss = jnp.maximum(logits, 0.0) + jnp.log1p(jnp.exp(-jnp.abs(logits))) - targets * logits
    totals[0] = jnp.sum(loss)
    totals[1] = jnp.sum(dlogit)
    totals_copy = pltpu.make_async_copy(totals, totals_hbm, small_sem.at[0])
    totals_copy.start()

    top = dlogit.astype(BF16).astype(F32)
    middle = (dlogit - top).astype(BF16).astype(F32)
    rest = dlogit - top - middle
    row = lax.broadcasted_iota(jnp.int32, (8, samples), 0)
    parts = jnp.where(row == 0, top, jnp.where(row == 1, middle, jnp.where(row == 2, rest, 0.0)))
    parts = jnp.concatenate([parts, parts], axis=1).astype(BF16)
    for c in range(CH):
        found = jnp.dot(parts, act_ref[c], preferred_element_type=F32)
        head[c:c + 1, :] = jnp.sum(found, axis=0, keepdims=True)
    head_copy = pltpu.make_async_copy(head, grad_head_hbm, small_sem.at[1])
    head_copy.start()
    for i in range(len(OUT_PARTS)):
        out_copy(i).wait()
    totals_copy.wait()
    head_copy.wait()


def per_device(genotypes, labels, gene_weight, gene_idx, head_weight, head_bias):
    samples = genotypes.shape[0]
    blocks = gene_weight.shape[0]
    genes = head_weight.shape[0]
    rows = genes + 2 * GSTR
    n = lax.axis_size("var")
    vmem = pl.BlockSpec(memory_space=pltpu.VMEM)
    hbm = pl.BlockSpec(memory_space=pltpu.HBM)
    smem = pl.BlockSpec(memory_space=pltpu.SMEM)
    shape = jax.ShapeDtypeStruct
    dma = pltpu.SemaphoreType.DMA
    pieces = len(split_blocks(blocks))
    parts = len(OUT_PARTS)
    stay = functools.partial(pltpu.with_memory_space_constraint, memory_space=pltpu.HBM)
    dose, spread, act, logit = pl.pallas_call(
        functools.partial(forward_kernel, n),
        out_shape=(
            shape((blocks * BLOCK, samples), BF16),
            shape((blocks, samples, SLOTS * CH), F32),
            shape((CH, 2 * samples, genes), BF16),
            shape((1, samples), F32),
        ),
        in_specs=[hbm] * 4,
        out_specs=(vmem,) * 4,
        scratch_shapes=[
            pltpu.VMEM((CH, blocks * SLOTS, samples), F32),
            pltpu.VMEM((SLOTS, gene_idx.shape[0]), jnp.int32),
            pltpu.VMEM((CH, genes), F32),
            pltpu.VMEM((samples, blocks * BLOCK), jnp.int32),
            pltpu.VMEM((blocks, BLOCK, SLOTS * CH), BF16),
            pltpu.VMEM((samples, blocks * BLOCK), BF16),
            pltpu.VMEM((CH, genes, samples), F32),
            pltpu.VMEM((CH, genes, samples), F32),
            pltpu.VMEM((CH, rows, samples), F32),
            pltpu.VMEM((2, CH * GSTR, samples), BF16),
            pltpu.VMEM((2, CH * GSTR, samples), BF16),
            pltpu.VMEM((2, CH * GSTR, samples), BF16),
            pltpu.VMEM((2, CH * GSTR, samples), BF16),
            pltpu.VMEM((CH, genes, samples), F32),
            pltpu.VMEM((8, samples), F32),
            pltpu.VMEM((1, 1, samples), F32),
            pltpu.VMEM((n, 1, samples), F32),
            dma((pieces,)), dma((pieces,)), dma((2,)),
            dma((2,)), dma((2,)), dma((2,)), dma((2,)),
            dma, dma,
        ],
        compiler_params=pltpu.CompilerParams(
            collective_id=0, has_side_effects=True, vmem_limit_bytes=24 * 1024 * 1024
        ),
        name="forward",
    )(stay(gene_idx.T), stay(head_weight.T), stay(genotypes), stay(gene_weight))
    grad_w, grad_head, totals = pl.pallas_call(
        backward_kernel,
        out_shape=(
            shape((blocks, BLOCK, SLOTS * CH), F32),
            shape((CH, genes), F32),
            shape((2,), F32),
        ),
        in_specs=[vmem, vmem, smem, vmem, vmem, vmem],
        out_specs=(hbm, hbm, hbm),
        scratch_shapes=[
            pltpu.VMEM((blocks, BLOCK, SLOTS * CH), F32),
            pltpu.VMEM((CH, genes), F32),
            pltpu.SMEM((2,), F32),
            dma((parts,)), dma((2,)),
        ],
        compiler_params=pltpu.CompilerParams(vmem_limit_bytes=24 * 1024 * 1024),
        name="backward",
    )(logit, labels.reshape(1, samples), head_bias, dose, spread, act)
    return (grad_w, grad_head.T, totals)


def solution(mesh):
    placed = (P("grp", "var"), P("grp"), P("var", None, None), P(), P("var", None), P())
    return jax.shard_map(
        per_device,
        mesh=mesh,
        in_specs=placed,
        out_specs=(P(("grp", "var"), None, None), P(("grp", "var"), None), P("grp")),
        check_vma=False,
    )
```
